128 devices in a mesh: dp: 8 (over z, y_hi), ctx: 16 (over x, y_lo, core).
Axes of the slice: x: 4, y: 4 (y_hi: 2, y_lo: 2; y = y_hi * 2 + y_lo), z: 4, core: 2. Of those that a mesh axis runs over, the one named last changes fastest.
Arguments:
- tokens: bfloat16 [8, 8192, 1024], P('dp', 'ctx'), may hold values from -60 to 60
- kept: int32 [8, 4096], P('dp', 'ctx'), may hold values from 0 to 8191, as said below
- gain_attn: float32 [1024], replicated, may hold values from 0.25 to 1.75
- gain_ffn: float32 [1024], replicated, may hold values from 0.25 to 1.75
- w_query: bfloat16 [1024, 1024], P(None, 'ctx'), may hold values from -4 to 4
- w_key: bfloat16 [1024, 1024], P(None, 'ctx'), may hold values from -4 to 4
- w_value: bfloat16 [1024, 1024], P(None, 'ctx'), may hold values from -0.1875 to 0.1875
- w_out: bfloat16 [1024, 1024], P('ctx'), may hold values from -0.1875 to 0.1875
- expert_ids: int32 [8, 4096, 1], P('dp', 'ctx'), may hold values from 0 to 127; in each aligned block of 256 rows (0 to 255, 256 to 511, ..., all dimensions but the last counted through in order) at most 4 rows name the same one
- w_in: bfloat16 [128, 1024, 2816], P(('dp', 'ctx')), may hold values from -0.1875 to 0.1875
- w_back: bfloat16 [128, 2816, 1024], P(('dp', 'ctx')), may hold values from -0.109375 to 0.109375
Outputs:
- blended: bfloat16 [8, 8192, 1024], P('dp', 'ctx')
The draws below stay inside these ranges and needn't reach their ends.
Inputs may be any that keep to these rules, and one draw needn't show every extreme that they name: `kept`: in each document row, entries j * 256 to (j + 1) * 256 - 1 are strictly increasing positions from j * 512 to (j + 1) * 512 - 1. `expert_ids`: in each aligned block of 256 rows (the kept positions of one block b) no expert is named more than 4 times.
All inputs are finite; a program needn't handle non-finite values.
Results may differ from the reference program's by a relative error of at most 0.007.
Values may be sent and summed in bfloat16 or wider, within the bound.
No kernel may reach another device: no remote copies, remote signals or barrier semaphores. Data moves between devices by JAX's collectives and lax.ppermute only.
A program may use at most 64 MiB of HBM per device.

```python
import math
import jax
import jax.numpy as jnp
import numpy as np
from jax import lax

D = 1024
HS = 64
FF = 2816
SHARD_DEV = 512
HEADS = 16
EXPERTS = 128
INNER = 1024
KEEP_DEV = 256
KEEP = 4096
SEQ = 8192
DOCS = 8
CAP = 4
DEVICES = 128


def draw_tokens(key, part):
    noise = jax.random.normal(jax.random.fold_in(key, 1), (DOCS, SEQ, D), jnp.float32)
    return jnp.clip(noise, -6.0, 6.0).astype(jnp.bfloat16)


def draw_projection(key, salt):
    base = jax.random.normal(jax.random.fold_in(key, salt), (D, INNER), jnp.float32) / math.sqrt(D)
    return jnp.clip(base, -4.0, 4.0).astype(jnp.bfloat16)


def draw_w_query(key, part):
    return draw_projection(key, 3)


def draw_w_key(key, part):
    return draw_projection(key, 4)


def draw_kept(key, part):
    shards = SEQ // SHARD_DEV
    streams = jax.random.split(jax.random.fold_in(key, 5), DOCS * shards)

    def choose_some(stream):
        return jnp.sort(jax.random.permutation(stream, SHARD_DEV)[:KEEP_DEV].astype(jnp.int32))
    chosen = jax.vmap(choose_some)(streams).reshape(DOCS, shards, KEEP_DEV)
    offsets = (jnp.arange(shards, dtype=jnp.int32) * SHARD_DEV)[None, :, None]
    return (chosen + offsets).reshape(DOCS, KEEP).astype(jnp.int32)


def level_of(stream_key, shape, cuts, smallest, largest):
    level = 1.0
    for dim, parts in cuts:
        draws = jax.random.uniform(jax.random.fold_in(jax.random.fold_in(stream_key, 6), dim), (parts,), jnp.float32, smallest / len(cuts), largest / len(cuts))
        level = level * jnp.repeat(jnp.exp(draws), shape[dim] // parts).reshape((-1,) + (1,) * (len(shape) - 1 - dim))
    return level


def deal_out(own_key, own, number, rows, count, top, limit, skew):
    order = jax.random.permutation(own_key, count)
    crowded, ordinary = shares(count, rows * top, limit, skew, True), shares(count, rows * top, limit, skew, False)
    places = jnp.arange(count)

    def named(tallies, offset_by):
        used = int((tallies > 0).sum())
        fixed = max(1, used // 4)
        shifted = fixed + (places - fixed + offset_by * (used - fixed)) % max(1, count - fixed)
        return jnp.zeros((count,), jnp.int32).at[order[jnp.where(places < fixed, places, shifted)]].set(jnp.asarray(tallies, jnp.int32))

    tallies = jnp.where(number % 4 == 0, named(crowded, number // 4), named(ordinary, number - number // 4 - 1))
    mixed = jax.random.permutation(jax.random.fold_in(own, 3), count)
    donor, taker = mixed[0:count // 2 * 2:2], mixed[1:count // 2 * 2:2]
    room = jnp.minimum(tallies[donor] - 1, limit - tallies[taker]) // 2
    room = jnp.where((donor == order[0]) | (taker == order[0]) | (tallies[taker] == 0), 0, jnp.maximum(room, 0))
    shifted = jax.random.randint(jax.random.fold_in(own, 4), (count // 2,), 0, 1 << 20) % (room + 1)
    tallies = tallies.at[donor].add(-shifted).at[taker].add(shifted)
    labels = jnp.searchsorted(jnp.cumsum(tallies), jnp.arange(rows * top), side="right").astype(jnp.int32)
    table = labels.reshape(top, rows).T
    table = table[jax.random.permutation(jax.random.fold_in(own, 1), rows)]
    offset_by = jax.random.randint(jax.random.fold_in(own, 2), (rows, 1), 0, top)
    return jnp.take_along_axis(table, (jnp.arange(top)[None, :] + offset_by) % top, axis=1)


def shares(number_of, total, most, skew, full):
    portions = [(1 << 20) // math.isqrt(standing ** skew) + 1 for standing in range(1, number_of + 1)]
    largest = most if full else min(most, max(-(-total // number_of), total * portions[0] // sum(portions)))
    least = 1 if total - largest >= number_of - 1 else 0
    holding, rest = [largest] + [least] * (number_of - 1), total - largest - least * (number_of - 1)
    while rest > 0:
        movable = [i for i in range(1, number_of) if holding[i] < largest] or [i for i in range(1, number_of) if holding[i] < most]
        whole, budget = sum([portions[i] for i in movable]), rest
        for i in movable:
            addition = min(most - holding[i], max(1, budget * portions[i] // whole), rest)
            holding[i] = holding[i] + addition
            rest = rest - addition
    return np.array(holding)


def normal_values(stream_key, shape, deviation, limit, cuts=(), kind=jnp.bfloat16):
    level = level_of(stream_key, shape, cuts, -0.22, 0.18) if cuts else 1.0
    values = jax.random.normal(stream_key, shape, jnp.float32) * deviation * level
    return jnp.minimum(jnp.maximum(values, -limit), limit).astype(kind)


def setup_inputs(seed: int = 0) -> dict:
    splits = jax.random.split(jax.random.key(seed), 12)
    tokens = draw_tokens(jax.random.fold_in(splits[11], 71), 0)
    kept = draw_kept(jax.random.fold_in(splits[11], 71), 0)
    gain_attn = jnp.clip(1.0 + 0.15 * jax.random.normal(splits[2], (D,), jnp.float32), 0.25, 1.75)
    gain_ffn = jnp.clip(1.0 + 0.15 * jax.random.normal(splits[3], (D,), jnp.float32), 0.25, 1.75)
    w_query = draw_w_query(jax.random.fold_in(splits[11], 71), 0)
    w_key = draw_w_key(jax.random.fold_in(splits[11], 71), 0)
    w_value = normal_values(splits[6], (D, INNER), D ** -0.5, 0.1875, ((1, 16),))
    w_out = normal_values(splits[7], (INNER, D), INNER ** -0.5, 0.1875, ((0, 16),))
    expert_ids_keys = jax.random.split(jax.random.fold_in(splits[8], 1), DOCS * KEEP // KEEP_DEV)
    expert_ids_turns = jax.random.permutation(jax.random.fold_in(splits[8], 3), DOCS * KEEP // KEEP_DEV)
    expert_ids = jax.vmap(lambda own, number: deal_out(jax.random.fold_in(splits[8], 2), own, number, KEEP_DEV, EXPERTS, 1, CAP, 1))(expert_ids_keys, expert_ids_turns).reshape((DOCS, KEEP, 1))
    w_in = normal_values(splits[9], (EXPERTS, D, FF), D ** -0.5, 0.1875, ((0, 128),))
    w_back = normal_values(splits[10], (EXPERTS, FF, D), FF ** -0.5, 0.109375, ((0, 128),))
    return {"tokens": tokens, "kept": kept, "gain_attn": gain_attn, "gain_ffn": gain_ffn, "w_query": w_query, "w_key": w_key, "w_value": w_value, "w_out": w_out, "expert_ids": expert_ids, "w_in": w_in, "w_back": w_back}


eps_norm = 1e-06
score_gain = 2.5

def rms_scale(values, gain):
    values = values.astype(jnp.float32)
    power = lax.optimization_barrier(jnp.mean(values * values, axis=-1, keepdims=True))
    return values * lax.rsqrt(power + eps_norm) * gain

def attend_document(triple):
    queries, keys, values = triple
    scale = score_gain / math.sqrt(HS)
    keys_wide = keys.astype(jnp.float32)
    values_wide = values.astype(jnp.float32)
    blocks = queries.reshape(KEEP // 512, 512, HEADS, HS)

    def one_block(block_rows):
        scores = jnp.einsum('qhd,khd->hqk', block_rows.astype(jnp.float32), keys_wide) * scale
        top = lax.optimization_barrier(jnp.max(scores, axis=-1, keepdims=True))
        weights = jnp.exp(scores - top)
        probs = (weights / lax.optimization_barrier(jnp.sum(weights, axis=-1, keepdims=True))).astype(jnp.bfloat16)
        mixed = jnp.einsum('hqk,khd->qhd', probs.astype(jnp.float32), values_wide)
        return mixed.astype(jnp.bfloat16)
    return lax.map(one_block, blocks).reshape(KEEP, HEADS * HS)

def reference(tokens, kept, gain_attn, gain_ffn, w_query, w_key, w_value, w_out, expert_ids, w_in, w_back):
    rows = jax.vmap(lambda doc, where: jnp.take(doc, where, axis=0))(tokens, kept)
    normed = rms_scale(rows, gain_attn).astype(jnp.bfloat16).reshape(DOCS * KEEP, D)
    queries = jnp.dot(normed, w_query, preferred_element_type=jnp.float32).astype(jnp.bfloat16)
    keys = jnp.dot(normed, w_key, preferred_element_type=jnp.float32).astype(jnp.bfloat16)
    values = jnp.dot(normed, w_value, preferred_element_type=jnp.float32).astype(jnp.bfloat16)
    shape4 = (DOCS, KEEP, HEADS, HS)
    mixed = lax.map(attend_document, (queries.reshape(shape4), keys.reshape(shape4), values.reshape(shape4)))
    attn = jnp.dot(mixed.reshape(DOCS * KEEP, INNER), w_out, preferred_element_type=jnp.float32)
    first = rows.reshape(DOCS * KEEP, D).astype(jnp.float32) + attn
    ffn_in = rms_scale(first, gain_ffn).astype(jnp.bfloat16)
    ids = expert_ids.reshape(DEVICES, KEEP_DEV).astype(jnp.int32)
    onehot = (ids[:, :, None] == jnp.arange(EXPERTS, dtype=jnp.int32)[None, None, :]).astype(jnp.int32)
    before = jnp.cumsum(onehot, axis=1) - onehot
    slots = lax.optimization_barrier(jnp.sum(before * onehot, axis=2)).astype(jnp.int32)
    place = (ids * CAP + slots).astype(jnp.int32)
    source = jnp.broadcast_to(jnp.arange(DEVICES, dtype=jnp.int32)[:, None], (DEVICES, KEEP_DEV))
    buffers = jnp.zeros((DEVICES, EXPERTS * CAP, D), jnp.bfloat16)
    buffers = buffers.at[source, place].set(ffn_in.reshape(DEVICES, KEEP_DEV, D))
    slabs = jnp.transpose(buffers.reshape(DEVICES, EXPERTS, CAP, D), (1, 0, 2, 3))

    def run_expert(args):
        slab, first_weight, second_weight = args
        flat_in = slab.reshape(DEVICES * CAP, D)
        hidden = jnp.maximum(jnp.dot(flat_in, first_weight, preferred_element_type=jnp.float32), 0.0)
        hidden = hidden.astype(jnp.bfloat16)
        answer = jnp.dot(hidden, second_weight, preferred_element_type=jnp.float32).astype(jnp.bfloat16)
        return answer.reshape(DEVICES, CAP, D)
    answers = lax.map(run_expert, (slabs, w_in, w_back))
    back = jnp.transpose(answers, (1, 0, 2, 3)).reshape(DEVICES, EXPERTS * CAP, D)
    taken = jnp.take_along_axis(back, place[:, :, None], axis=1)
    second = (first + taken.reshape(DOCS * KEEP, D).astype(jnp.float32)).astype(jnp.bfloat16)
    second = second.reshape(DOCS, KEEP, D)
    return jax.vmap(lambda doc, where, fresh: doc.at[where].set(fresh))(tokens, kept, second)
```

```python
import math

import jax
import jax.numpy as jnp
from jax import lax
from jax.sharding import PartitionSpec as P

HS = 64


eps_norm = 1e-06
score_gain = 2.5


def rms_scale(values, gain):
    values = values.astype(jnp.float32)
    power = jnp.mean(values * values, axis=-1, keepdims=True)
    return values * lax.rsqrt(power + eps_norm) * gain


def attend(queries, keys, values):
    count, heads_here, width = queries.shape
    block = 512
    scale = score_gain / math.sqrt(width)
    blocks = queries.reshape(count // block, block, heads_here, width)

    def one_block(block_rows):
        scores = (
            jnp.einsum("qhd,khd->hqk", block_rows, keys, preferred_element_type=jnp.float32) * scale
        )
        top = jnp.max(scores, axis=-1, keepdims=True)
        weights = jnp.exp(scores - top)
        probs = (weights / jnp.sum(weights, axis=-1, keepdims=True)).astype(jnp.bfloat16)
        mixed = jnp.einsum("hqk,khd->qhd", probs, values, preferred_element_type=jnp.float32)
        return mixed.astype(jnp.bfloat16)

    return lax.map(one_block, blocks).reshape(count, heads_here, width)


def body(
    tokens, kept, gain_attn, gain_ffn, w_query, w_key, w_value, w_out, expert_ids, w_in, w_back
):
    document = tokens[0]
    shard_len, width_model = document.shape
    ctx_count = lax.axis_size("ctx")
    dp_count = lax.axis_size("dp")
    local = kept[0] - lax.axis_index("ctx") * shard_len
    rows = jnp.take(document, local, axis=0)
    keep_here = rows.shape[0]
    normed = rms_scale(rows, gain_attn).astype(jnp.bfloat16)
    head_width = HS
    heads_here = w_query.shape[1] // head_width
    stacked = jnp.stack([w_query, w_key, w_value], axis=1)
    gathered = lax.all_gather(normed, "ctx", axis=0, tiled=True)
    triple = jnp.einsum(
        "td,dcf->tcf",
        gathered,
        stacked,
        preferred_element_type=jnp.float32,
    ).astype(jnp.bfloat16)
    triple = triple.reshape(triple.shape[0], 3, heads_here, head_width)
    mixed = attend(triple[:, 0], triple[:, 1], triple[:, 2])
    flat_mixed = mixed.reshape(mixed.shape[0], heads_here * head_width)
    parts = lax.all_to_all(
        flat_mixed.reshape(ctx_count, keep_here, heads_here * head_width),
        "ctx",
        split_axis=0,
        concat_axis=0,
        tiled=True,
    )
    w_rows, _ = lax.optimization_barrier((w_out, gathered))
    w_all = lax.all_gather(w_rows, "ctx", axis=0, tiled=True)
    mine = jnp.transpose(parts, (1, 0, 2)).reshape(keep_here, -1)
    attn = jnp.dot(mine, w_all, preferred_element_type=jnp.float32)
    first = rows.astype(jnp.float32) + attn
    ffn_in = rms_scale(first, gain_ffn).astype(jnp.bfloat16)
    expert_here = w_in.shape[0]
    owners = dp_count * ctx_count
    experts_all = expert_here * owners
    capacity = 2 * keep_here // experts_all
    labels = expert_ids[0, :, 0]
    choose = (labels[:, None] == jnp.arange(experts_all, dtype=jnp.int32)[None, :]).astype(
        jnp.float32
    )
    order = jnp.arange(keep_here, dtype=jnp.int32)
    earlier = (order[None, :] < order[:, None]).astype(jnp.float32)
    before = jnp.dot(earlier, choose, precision=lax.Precision.HIGHEST)
    slots = jnp.sum(before * choose, axis=1).astype(jnp.int32)
    place = labels * capacity + slots
    spots = (place[None, :] == jnp.arange(experts_all * capacity, dtype=jnp.int32)[:, None]).astype(
        jnp.bfloat16
    )
    buffer = jnp.dot(spots, ffn_in, preferred_element_type=jnp.float32).astype(jnp.bfloat16)
    buffer = buffer.reshape(experts_all, capacity, width_model)
    received = lax.all_to_all(buffer, ("dp", "ctx"), split_axis=0, concat_axis=0, tiled=True)
    items = received.shape[1]
    grouped = received.reshape(owners, expert_here, items, width_model)
    hidden = jnp.einsum("sgid,gdf->sgif", grouped, w_in, preferred_element_type=jnp.float32)
    hidden = jnp.maximum(hidden, 0.0).astype(jnp.bfloat16)
    answer = jnp.einsum("sgif,gfd->sgid", hidden, w_back, preferred_element_type=jnp.float32)
    answered = answer.astype(jnp.bfloat16).reshape(owners * expert_here, items, width_model)
    back = lax.all_to_all(answered, ("dp", "ctx"), split_axis=0, concat_axis=0, tiled=True)
    answers = back.reshape(experts_all * capacity, width_model)
    taken = jnp.take(answers, place, axis=0)
    second = (first + taken.astype(jnp.float32)).astype(jnp.bfloat16)
    blended = document.at[local].set(second)
    return blended[None]


def solution(mesh):
    return jax.shard_map(
        body,
        mesh=mesh,
        in_specs=(
            P("dp", "ctx", None),
            P("dp", "ctx"),
            P(),
            P(),
            P(None, "ctx"),
            P(None, "ctx"),
            P(None, "ctx"),
            P("ctx", None),
            P("dp", "ctx", None),
            P(("dp", "ctx"), None, None),
            P(("dp", "ctx"), None, None),
        ),
        out_specs=P("dp", "ctx", None),
        check_vma=False,
    )
```

```python
import functools
import math

import jax
import jax.numpy as jnp
from jax import lax
from jax.experimental import pallas as pl
from jax.experimental.pallas import tpu as pltpu
from jax.sharding import PartitionSpec as P

HS = 64
LANES = 128
HALF = 128
SLOTS = 4
eps_norm = 1e-06
score_gain = 2.5
SCALE2 = score_gain / math.sqrt(HS) * math.log2(math.e)

A0, A1, A2, A3 = (0, 0), (1, 0), (2, 0), (3, 0)
B0, B1, B2, B3 = (0, 1), (1, 1), (2, 1), (3, 1)
UNITS = (
    [(c, h) for c in (A0, A3, A1, B0) for h in (0, 1)]
    + [(A2, 0), (B3, 0), (A2, 1), (B1, 0), (B1, 1), (B3, 1)]
    + [(B2, 0), (B2, 1)]
)


def params(limit=48):
    return pltpu.CompilerParams(vmem_limit_bytes=limit << 20)


def cost(flops, moved, exps=0):
    return pl.CostEstimate(flops=int(flops), bytes_accessed=int(moved), transcendentals=int(exps))


def dot32(a, b):
    return jnp.dot(a, b, preferred_element_type=jnp.float32)


def dot_first(a, b):
    return lax.dot_general(a, b, (((0,), (0,)), ((), ())), preferred_element_type=jnp.float32)


def iota(shape, axis):
    return lax.broadcasted_iota(jnp.int32, shape, axis)


def one_hot(flag):
    return jnp.where(flag, 1.0, 0.0).astype(jnp.bfloat16)


def rms_scale(values, gain):
    power = jnp.mean(values * values, axis=-1, keepdims=True)
    return values * lax.rsqrt(power + eps_norm) * gain


def gather_kernel(local_ref, doc_ref, gain_ref, rows_ref, normed_ref):
    local = local_ref[...]
    spread = one_hot(iota((doc_ref.shape[0], local.shape[1]), 0) == local)
    rows = dot_first(spread, doc_ref[...])
    rows_ref[...] = rows.astype(jnp.bfloat16)
    normed_ref[...] = rms_scale(rows, gain_ref[...]).astype(jnp.bfloat16)


def gather_rows(local, document, gain):
    keep, (_, width) = local.shape[1], document.shape
    shape = jax.ShapeDtypeStruct((keep, width), jnp.bfloat16)
    return pl.pallas_call(
        gather_kernel,
        out_shape=(shape, shape),
        compiler_params=params(),
        cost_estimate=cost(2 * keep * document.size, 2 * (document.size + 2 * keep * width)),
        name="gather_rows",
    )(local, document, gain)


def project_kernel(*refs):
    *blocks, own_w, other_w, own_ref, other_ref = refs
    at = 0
    for block in blocks:
        here = pl.ds(at, block.shape[0])
        value = block[...]
        own_ref[here, :] = dot32(value, own_w[...]).astype(jnp.bfloat16)
        other_ref[here, :] = dot32(value, other_w[...]).astype(jnp.bfloat16)
        at += block.shape[0]


def project(blocks, own_w, other_w):
    count = sum(block.shape[0] for block in blocks)
    shape = jax.ShapeDtypeStruct((count, own_w.shape[1]), jnp.bfloat16)
    depth = own_w.shape[0]
    return pl.pallas_call(
        project_kernel,
        out_shape=(shape, shape),
        compiler_params=params(),
        cost_estimate=cost(4 * count * own_w.size, 2 * (count * depth + 2 * own_w.size)),
        name="project_rows",
    )(*blocks, own_w, other_w)


def attend_kernel(where_ref, *refs, pieces, chunk, span):
    packed, (out_ref, keys, values, queries, mixed) = refs[:pieces], refs[pieces:]
    step = pl.program_id(0)
    total = keys.shape[1]

    @pl.when(step == 0)
    def _():
        at = 0
        for piece in packed:
            count = piece.shape[0]
            here = pl.ds(at, count)
            pair = piece[:, :LANES].astype(jnp.float32)
            lane = iota((count, LANES), 1)
            twice = jnp.where(lane < HS, pair, pltpu.roll(pair, HS, 1)) * SCALE2
            high = twice.astype(jnp.bfloat16).astype(jnp.float32)
            queries[here, :] = jnp.where(lane < HS, high, twice - high).astype(jnp.bfloat16)
            turned = pair.T[HS:, :].astype(jnp.bfloat16)
            keys[:HS, here] = turned
            keys[HS:, here] = turned
            ones = jnp.where(lane == HS, 1.0, 0.0)
            values[here, :] = (piece[:, LANES:].astype(jnp.float32) + ones).astype(jnp.bfloat16)
            at += count

    query = queries[pl.ds(pl.multiple_of(step * span, span), span), :]
    top = jnp.full((span, 1), -1e30, jnp.float32)
    held = jnp.zeros((span, LANES), jnp.float32)
    for j in range(total // chunk):
        here = pl.ds(j * chunk, chunk)
        scores = dot32(query, keys[:, here])
        newer = jnp.maximum(top, jnp.max(scores, axis=1, keepdims=True))
        weights = jnp.exp2(scores - newer).astype(jnp.bfloat16)
        held = held * jnp.exp2(top - newer) + dot32(weights, values[here, :])
        top = newer
    mixed[...] = held.T
    result = (mixed[:HS, :] / mixed[HS : HS + 1, :]).astype(jnp.bfloat16)
    units = span // HALF
    for first in range(total // span):

        @pl.when(step == first)
        def _():
            for k in range(units):
                unit = first * units + k
                half = UNITS[unit % len(UNITS)][1]
                out_ref[where_ref[unit], :, half * HALF : (half + 1) * HALF] = result[
                    :, k * HALF : (k + 1) * HALF
                ]


def attend(where, packed, blocks):
    total = sum(piece.shape[0] for piece in packed)
    span, chunk = 1024, 512
    return pl.pallas_call(
        functools.partial(attend_kernel, pieces=len(packed), chunk=chunk, span=span),
        grid_spec=pltpu.PrefetchScalarGridSpec(
            num_scalar_prefetch=1,
            grid=(total // span,),
            in_specs=[pl.BlockSpec(piece.shape, lambda i, w: (0, 0)) for piece in packed],
            out_specs=pl.BlockSpec((blocks, HS, 2 * HALF), lambda i, w: (0, 0, 0)),
            scratch_shapes=[
                pltpu.VMEM((LANES, total), jnp.bfloat16),
                pltpu.VMEM((total, LANES), jnp.bfloat16),
                pltpu.VMEM((total, LANES), jnp.bfloat16),
                pltpu.VMEM((LANES, span), jnp.float32),
            ],
        ),
        out_shape=jax.ShapeDtypeStruct((blocks, HS, 2 * HALF), jnp.bfloat16),
        compiler_params=params(),
        cost_estimate=cost(4 * total * total * LANES, 6 * total * LANES, total * total),
        name="attend_heads",
    )(where, *packed)


def dispatch_kernel(mixed_ref, w_ref, rows_ref, gain_ref, label_ref, first_ref, send_ref, place_ref):
    first = rows_ref[...].astype(jnp.float32) + dot_first(mixed_ref[...], w_ref[...])
    first_ref[...] = first
    entry = rms_scale(first, gain_ref[...]).astype(jnp.bfloat16)
    keep, width = first.shape
    label = label_ref[...].astype(jnp.float32)
    across = jnp.broadcast_to(label, (keep, keep))
    same = (across == across.T) & (iota((keep, keep), 0) < iota((keep, keep), 1))
    slot = jnp.sum(jnp.where(same, 1.0, 0.0), axis=0, keepdims=True)
    place = (label * (2 * SLOTS) + slot).astype(jnp.int32)
    place_ref[...] = place
    places = send_ref.shape[0]
    half = width // 2
    row = iota((places, keep), 0)
    send = dot32(one_hot(row == place), entry[:, :half])
    send = send + dot32(one_hot(row == place + SLOTS), entry[:, half:])
    send_ref[...] = send.astype(jnp.bfloat16)


def dispatch(mixed, w_all, rows, gain, label, experts):
    keep, width = rows.shape
    places = experts * 2 * SLOTS
    return pl.pallas_call(
        dispatch_kernel,
        out_shape=(
            jax.ShapeDtypeStruct((keep, width), jnp.float32),
            jax.ShapeDtypeStruct((places, width // 2), jnp.bfloat16),
            jax.ShapeDtypeStruct((1, keep), jnp.int32),
        ),
        compiler_params=params(),
        cost_estimate=cost(4 * keep * w_all.size, 2 * w_all.size + 10 * keep * width),
        name="dispatch_rows",
    )(mixed, w_all, rows, gain, label)


def expert_kernel(slots_ref, w_in_ref, w_back_ref, out_ref, entry, total):
    step = pl.program_id(0)
    count, half = slots_ref.shape
    pairs = count // 16

    @pl.when(step == 0)
    def _():
        got = slots_ref[...].astype(jnp.float32).reshape(pairs, 2, 8, half)
        even, odd = got[:, 0], got[:, 1]
        low_side = iota((pairs, 8, half), 1) < SLOTS
        low = jnp.where(low_side, even, pltpu.roll(odd, SLOTS, 1))
        high = jnp.where(low_side, pltpu.roll(even, SLOTS, 1), odd)
        entry[:, :half] = low.reshape(count // 2, half).astype(jnp.bfloat16)
        entry[:, half:] = high.reshape(count // 2, half).astype(jnp.bfloat16)

    hidden = jnp.maximum(dot32(entry[...], w_in_ref[...]), 0.0).astype(jnp.bfloat16)
    part = dot32(hidden, w_back_ref[...])

    @pl.when(step == 0)
    def _():
        total[...] = part

    @pl.when(step > 0)
    def _():
        total[...] += part

    @pl.when(step == pl.num_programs(0) - 1)
    def _():
        low = total[:, :half].reshape(pairs, 8, half)
        high = total[:, half:].reshape(pairs, 8, half)
        low_side = iota((pairs, 8, half), 1) < SLOTS
        even = jnp.where(low_side, low, pltpu.roll(high, SLOTS, 1))
        odd = jnp.where(low_side, pltpu.roll(low, SLOTS, 1), high)
        both = jnp.concatenate([even[:, None], odd[:, None]], axis=1)
        out_ref[...] = both.reshape(count, half).astype(jnp.bfloat16)


def run_expert(slots, w_in, w_back):
    count, half = slots.shape
    width, inner = w_in.shape
    tile = 256
    return pl.pallas_call(
        expert_kernel,
        grid=(inner // tile,),
        in_specs=[
            pl.BlockSpec((count, half), lambda i: (0, 0)),
            pl.BlockSpec((width, tile), lambda i: (0, i)),
            pl.BlockSpec((tile, width), lambda i: (i, 0)),
        ],
        out_specs=pl.BlockSpec((count, half), lambda i: (0, 0)),
        out_shape=jax.ShapeDtypeStruct((count, half), jnp.bfloat16),
        scratch_shapes=[
            pltpu.VMEM((count // 2, width), jnp.bfloat16),
            pltpu.VMEM((count // 2, width), jnp.float32),
        ],
        compiler_params=params(),
        cost_estimate=cost(2 * count * w_in.size, 4 * w_in.size + 4 * slots.size),
        name="run_expert",
    )(slots, w_in, w_back)


def combine_kernel(back_ref, place_ref, first_ref, local_ref, doc_ref, out_ref):
    back = back_ref[...]
    places, half = back.shape
    place = place_ref[...]
    keep = place.shape[1]
    row = iota((places, keep), 0)
    low = dot_first(one_hot(row == place), back)
    high = dot_first(one_hot(row == place + SLOTS), back)
    taken = jnp.concatenate([low, high], axis=1)
    second = (first_ref[...] + taken).astype(jnp.bfloat16)
    spread = iota((doc_ref.shape[0], keep), 0) == local_ref[...]
    fresh = dot32(one_hot(spread), second).astype(jnp.bfloat16)
    hit = jnp.max(jnp.where(spread, 1.0, 0.0), axis=1, keepdims=True) > 0.5
    out_ref[...] = jnp.where(hit, fresh, doc_ref[...])


def combine(back, place, first, local, document):
    keep, width = first.shape
    return pl.pallas_call(
        combine_kernel,
        out_shape=jax.ShapeDtypeStruct(document.shape, document.dtype),
        compiler_params=params(),
        cost_estimate=cost(2 * keep * (2 * back.size + document.size), 6 * document.size),
        name="combine_rows",
    )(back, place, first, local, document)


def body(
    tokens, kept, gain_attn, gain_ffn, w_query, w_key, w_value, w_out, expert_ids, w_in, w_back
):
    document = tokens[0]
    shard_len, width = document.shape
    ctx_count = lax.axis_size("ctx")
    experts = lax.axis_size("dp") * ctx_count
    me = lax.axis_index("ctx")
    keep = kept.shape[1]
    local = kept - me * shard_len

    def along(value, step):
        pairs = [(i, (i // 4 + step) % 4 * 4 + i % 4) for i in range(ctx_count)]
        return lax.ppermute(value, "ctx", pairs)

    def flip(value, bit):
        return lax.ppermute(value, "ctx", [(i, i ^ bit) for i in range(ctx_count)])

    own_w = jnp.concatenate([w_query, w_key, w_value, jnp.zeros_like(w_value)], axis=1)
    other_w = flip(own_w, 1)
    w_all = lax.all_gather(w_out, "ctx", axis=0, tiled=True)
    rows, normed = gather_rows(local, document, gain_attn[None])

    a3, a1, b0 = along(normed, 1), along(normed, 3), flip(normed, 2)
    r1 = along(jnp.concatenate([a3[:HALF], b0[:HALF]]), 1)
    r2 = along(jnp.concatenate([a1[HALF:], b0[:HALF]]), 3)
    r3 = flip(jnp.concatenate([a1[HALF:], a3[HALF:]]), 2)
    b2 = flip(jnp.concatenate([r1[:HALF], r2[:HALF]]), 2)
    stages = [[normed], [a3, a1, b0], [r1, r2, r3], [b2]]
    own, other = [], []
    for blocks in stages:
        mine, theirs = project(blocks, own_w, other_w)
        own.append(mine)
        other.append(flip(theirs, 1))

    def places(core):
        found = []
        for (dx, dy), _ in UNITS:
            x, y = (me // 4 + dx) % 4, (me // 2 % 2) ^ dy
            found.append(x * 4 + y * 2 + core)
        return found

    core = me % 2
    where = jnp.stack(places(core) + places(1 - core)).astype(jnp.int32)
    mixed = attend(where, own + other, ctx_count)
    parts = lax.all_to_all(mixed, "ctx", split_axis=0, concat_axis=0, tiled=True)

    label = expert_ids[:, :, 0]
    first, send, place = dispatch(
        parts.reshape(-1, keep), w_all, rows, gain_ffn[None], label, experts
    )
    names = ("dp", "ctx")
    send = send.reshape(experts, 2 * SLOTS, width // 2)
    got = lax.all_to_all(send, names, split_axis=0, concat_axis=0, tiled=True)
    answer = run_expert(got.reshape(-1, width // 2), w_in[0], w_back[0])
    answer = answer.reshape(experts, 2 * SLOTS, width // 2)
    back = lax.all_to_all(answer, names, split_axis=0, concat_axis=0, tiled=True)
    return combine(back.reshape(-1, width // 2), place, first, local, document)[None]


def solution(mesh):
    return jax.shard_map(
        body,
        mesh=mesh,
        in_specs=(
            P("dp", "ctx", None),
            P("dp", "ctx"),
            P(),
            P(),
            P(None, "ctx"),
            P(None, "ctx"),
            P(None, "ctx"),
            P("ctx", None),
            P("dp", "ctx", None),
            P(("dp", "ctx"), None, None),
            P(("dp", "ctx"), None, None),
        ),
        out_specs=P("dp", "ctx", None),
        check_vma=False,
    )
```

```python
import functools
import math

import jax
import jax.numpy as jnp
from jax import lax
from jax.experimental import pallas as pl
from jax.experimental.pallas import tpu as pltpu
from jax.sharding import PartitionSpec as P

HS = 64
LANES = 128
HALF = 128
SLOTS = 4
eps_norm = 1e-06
score_gain = 2.5
SCALE2 = score_gain / math.sqrt(HS) * math.log2(math.e)

A0, A1, A2, A3 = (0, 0), (1, 0), (2, 0), (3, 0)
B0, B1, B2, B3 = (0, 1), (1, 1), (2, 1), (3, 1)
EARLY = [(c, h) for c in (A0, A3, A1, B0) for h in (0, 1)]
LATE = [(A2, 0), (B3, 0), (A2, 1), (B1, 0), (B1, 1), (B3, 1), (B2, 0), (B2, 1)]
THIRD, REST = 96, 176


def params(limit):
    return pltpu.CompilerParams(vmem_limit_bytes=limit << 20)


def cost(flops, moved, exps=0):
    return pl.CostEstimate(flops=int(flops), bytes_accessed=int(moved), transcendentals=int(exps))


def dot32(a, b):
    return jnp.dot(a, b, preferred_element_type=jnp.float32)


def dot_first(a, b):
    return lax.dot_general(a, b, (((0,), (0,)), ((), ())), preferred_element_type=jnp.float32)


def iota(shape, axis):
    return lax.broadcasted_iota(jnp.int32, shape, axis)


def one_hot(flag):
    return jnp.where(flag, 1.0, 0.0).astype(jnp.bfloat16)


def rms_scale(values, gain):
    power = jnp.mean(values * values, axis=-1, keepdims=True)
    return values * lax.rsqrt(power + eps_norm) * gain


def gather_kernel(*refs):
    sources, (rows_hbm, normed_ref, w_ref), (kept, doc, gain, rows_ref, sems) = refs[:6], refs[6:9], refs[9:]
    head = sources[3].shape[0]
    targets = [kept, doc, gain] + [w_ref.at[k * head : (k + 1) * head, :] for k in range(3)]
    arrivals = [
        pltpu.make_async_copy(source, target, sems.at[k])
        for k, (source, target) in enumerate(zip(sources, targets))
    ]
    for arrival in arrivals:
        arrival.start()
    w_ref[3 * head :, :] = jnp.zeros((w_ref.shape[0] - 3 * head, w_ref.shape[1]), jnp.bfloat16)
    for arrival in arrivals:
        arrival.wait()
    length = doc.shape[0]
    spread = one_hot(iota((length, kept.shape[1]), 0) == kept[...] % length)
    rows = dot_first(spread, doc[...])
    rows_ref[...] = rows.astype(jnp.bfloat16)
    leaving = pltpu.make_async_copy(rows_ref, rows_hbm, sems.at[6])
    leaving.start()
    normed_ref[...] = rms_scale(rows, gain[...]).astype(jnp.bfloat16)
    leaving.wait()


def gather_rows(kept, document, gain, heads):
    keep, (_, width) = kept.shape[1], document.shape
    shape = jax.ShapeDtypeStruct((keep, width), jnp.bfloat16)
    vmem, hbm = pl.BlockSpec(memory_space=pltpu.VMEM), pl.BlockSpec(memory_space=pltpu.HBM)
    return pl.pallas_call(
        gather_kernel,
        in_specs=[hbm] * 6,
        out_specs=[hbm, vmem, vmem],
        out_shape=(shape, shape, jax.ShapeDtypeStruct((4 * HS, width), jnp.bfloat16)),
        scratch_shapes=[
            pltpu.VMEM(kept.shape, jnp.int32),
            pltpu.VMEM(document.shape, jnp.bfloat16),
            pltpu.VMEM(gain.shape, jnp.float32),
            pltpu.VMEM(shape.shape, jnp.bfloat16),
            pltpu.SemaphoreType.DMA((7,)),
        ],
        compiler_params=params(57),
        cost_estimate=cost(2 * keep * document.size, 2 * (document.size + 2 * keep * width)),
        name="gather_rows",
    )(kept, document, gain, *heads)


def rearrange_kernel(*refs, recipes):
    sources, outs = refs[: len(refs) - len(recipes)], refs[len(refs) - len(recipes) :]
    for out, recipe in zip(outs, recipes):
        at = 0
        for which, start, size in recipe:
            out[at : at + size, :] = sources[which][start : start + size, :]
            at += size


def rearrange(sources, recipes):
    width = sources[0].shape[1]
    rows = [sum(size for _, _, size in recipe) for recipe in recipes]
    return pl.pallas_call(
        functools.partial(rearrange_kernel, recipes=recipes),
        out_shape=[jax.ShapeDtypeStruct((count, width), jnp.bfloat16) for count in rows],
        compiler_params=params(8),
        cost_estimate=cost(0, 4 * sum(rows) * width),
        name="rearrange_rows",
    )(*sources)


def dot_last(a, b):
    return lax.dot_general(a, b, (((1,), (1,)), ((), ())), preferred_element_type=jnp.float32)


def project_kernel(*refs):
    *blocks, own_w, other_w, own_ref, other_ref = refs
    at = 0
    for block in blocks:
        here = pl.ds(at, block.shape[0])
        value = block[...]
        own_ref[here, :] = dot_last(value, own_w[...]).astype(jnp.bfloat16)
        other_ref[here, :] = dot_last(value, other_w[...]).astype(jnp.bfloat16)
        at += block.shape[0]


def project(blocks, own_w, other_w):
    count = sum(block.shape[0] for block in blocks)
    columns, depth = own_w.shape
    shape = jax.ShapeDtypeStruct((count, columns), jnp.bfloat16)
    return pl.pallas_call(
        project_kernel,
        out_shape=(shape, shape),
        compiler_params=params(8),
        cost_estimate=cost(4 * count * own_w.size, 2 * (count * depth + 2 * own_w.size)),
        name="project_rows",
    )(*blocks, own_w, other_w)


def unpack(packed, queries, keys, values):
    at = 0
    for piece in packed:
        count = piece.shape[0]
        here = pl.ds(at, count)
        pair = piece[:, :LANES].astype(jnp.float32)
        lane = iota((count, LANES), 1)
        twice = jnp.where(lane < HS, pair, pltpu.roll(pair, HS, 1)) * SCALE2
        high = twice.astype(jnp.bfloat16).astype(jnp.float32)
        queries[here, :] = jnp.where(lane < HS, high, twice - high).astype(jnp.bfloat16)
        turned = pair.T[HS:, :].astype(jnp.bfloat16)
        keys[:HS, here] = turned
        keys[HS:, here] = turned
        ones = jnp.where(lane == HS, 1.0, 0.0)
        values[here, :] = (piece[:, LANES:].astype(jnp.float32) + ones).astype(jnp.bfloat16)
        at += count


def chunks(total, size):
    return [(at, min(size, total - at)) for at in range(0, total, size)]


def online(query, top, held, stores, chunk):
    for keys, values in stores:
        for at, size in chunks(values.shape[0], chunk):
            scores = dot32(query, keys[:, at : at + size])
            newer = jnp.maximum(top, jnp.max(scores, axis=1, keepdims=True))
            weights = jnp.exp2(scores - newer).astype(jnp.bfloat16)
            held = held * jnp.exp2(top - newer) + dot32(weights, values[at : at + size, :])
            top = newer
    return top, held


def block_of(me, chip, side):
    dx, dy = chip
    x, y = me // 4, me // 2 % 2
    return (x + dx) % 4 * 4 + (1 - y if dy else y) * 2 + side


def attend_kernel(*refs, pieces, olds, last, spans):
    refs = list(refs)
    me = refs.pop(0)[0] if last else None
    packed, refs = refs[:pieces], refs[pieces:]
    stores = []
    for _ in range(olds):
        stores.append(refs[:3])
        refs = refs[3:]
    state = refs.pop(0) if olds else None
    out = refs.pop(0)
    queries, keys, values = refs[:3]
    turn = refs[3] if last else None
    unpack(packed, queries, keys, values)

    def finish(side, at, top, held, units):
        size = held.shape[0]
        if not last:
            lane = iota(held.shape, 1)
            out[pl.ds(at, size), :] = jnp.where(lane == HS + 1, top, held)
            return
        turned = held.T
        result = (turned[:HS] / turned[HS : HS + 1]).astype(jnp.bfloat16)
        core = me % 2
        side = jnp.where(side == 0, core, 1 - core)
        for k, (chip, half) in enumerate(units):
            out[block_of(me, chip, side), :, half * HALF : (half + 1) * HALF] = result[
                :, k * HALF : (k + 1) * HALF
            ]

    def each(total, size, step):
        def one(i, carry):
            step(i, pl.multiple_of(i * size, size))
            return carry

        lax.fori_loop(0, total // size, one, 0)

    for old_queries, _, _ in stores:

        def old_step(i, at):
            size = spans[0]
            held = state[pl.ds(at, size), :]
            query = old_queries[pl.ds(at, size), :]
            top = held[:, HS + 1 : HS + 2]
            finish(i, at, *online(query, top, held, [(keys, values)], 1024), EARLY)

        each(old_queries.shape[0], spans[0], old_step)
    seen = [(k, v) for _, k, v in stores] + [(keys, values)]

    def new_step(i, at):
        size = spans[-1]
        top = jnp.full((size, 1), -1e30, jnp.float32)
        held = jnp.zeros((size, LANES), jnp.float32)
        finish(i, at, *online(queries[pl.ds(at, size), :], top, held, seen, 1024), LATE)

    each(queries.shape[0], spans[-1], new_step)


def attend(packed, stores, state, spans, me=None, blocks=0):
    fresh = sum(piece.shape[0] for piece in packed)
    old = sum(store[0].shape[0] for store in stores)
    last = me is not None
    kept_shapes = [(fresh, LANES), (LANES, fresh), (fresh, LANES)]
    vmem = pl.BlockSpec(memory_space=pltpu.VMEM)
    operands = list(packed) + [value for store in stores for value in store]
    operands += [state] if stores else []
    in_specs = [vmem] * len(operands)
    if last:
        operands, in_specs = [me] + operands, [pl.BlockSpec(memory_space=pltpu.SMEM)] + in_specs
        out_shape = jax.ShapeDtypeStruct((blocks, HS, 2 * HALF), jnp.bfloat16)
        scratch = [pltpu.VMEM(shape, jnp.bfloat16) for shape in kept_shapes]
        scratch.append(pltpu.VMEM((LANES, max(spans)), jnp.float32))
        out_specs = vmem
    else:
        out_shape = [jax.ShapeDtypeStruct((old + fresh, LANES), jnp.float32)]
        out_shape += [jax.ShapeDtypeStruct(shape, jnp.bfloat16) for shape in kept_shapes]
        scratch = []
        out_specs = [vmem] * 4
    pairs = old * fresh + fresh * (old + fresh)
    return pl.pallas_call(
        functools.partial(
            attend_kernel,
            pieces=len(packed),
            olds=len(stores),
            last=last,
            spans=spans,
        ),
        in_specs=in_specs,
        out_specs=out_specs,
        out_shape=out_shape,
        scratch_shapes=scratch,
        compiler_params=params(24),
        cost_estimate=cost(16 * pairs * LANES, 16 * (old + fresh) * LANES, pairs),
        name="attend_heads",
    )(*operands)


def dispatch_kernel(
    me_ref, mixed_ref, near_ref, far_ref, rows_ref, gain_ref, label_ref, first_ref, send_ref, place_ref, mixed
):
    blocks, head, _ = mixed_ref.shape
    me = me_ref[0]
    for k in range(blocks):
        chip = (k // 2 % 4, k % 2)
        side = me % 2 if k < blocks // 2 else 1 - me % 2
        mixed[k * head : (k + 1) * head, :] = mixed_ref[block_of(me, chip, side)]
    inner = near_ref.shape[0]
    first = dot_first(mixed[:inner, :], near_ref[...]) + dot_first(mixed[inner:, :], far_ref[...])
    first = rows_ref[...].astype(jnp.float32) + first
    first_ref[...] = first
    entry = rms_scale(first, gain_ref[...]).astype(jnp.bfloat16)
    keep, width = first.shape
    label = label_ref[...].astype(jnp.float32)
    across = jnp.broadcast_to(label, (keep, keep))
    same = (across == across.T) & (iota((keep, keep), 0) < iota((keep, keep), 1))
    slot = jnp.sum(jnp.where(same, 1.0, 0.0), axis=0, keepdims=True)
    place = (label * (2 * SLOTS) + slot).astype(jnp.int32)
    place_ref[...] = place
    places = send_ref.shape[0]
    half = width // 2
    row = iota((places, keep), 0)
    send = dot32(one_hot(row == place), entry[:, :half])
    send = send + dot32(one_hot(row == place + SLOTS), entry[:, half:])
    send_ref[...] = send.astype(jnp.bfloat16)


def dispatch(me, mixed, near, far, rows, gain, label, experts):
    keep, width = rows.shape
    places = experts * 2 * SLOTS
    vmem = pl.BlockSpec(memory_space=pltpu.VMEM)
    return pl.pallas_call(
        dispatch_kernel,
        in_specs=[pl.BlockSpec(memory_space=pltpu.SMEM)] + [vmem] * 6,
        scratch_shapes=[pltpu.VMEM((mixed.shape[0] * mixed.shape[1], keep), jnp.bfloat16)],
        out_shape=(
            jax.ShapeDtypeStruct((keep, width), jnp.float32),
            jax.ShapeDtypeStruct((places, width // 2), jnp.bfloat16),
            jax.ShapeDtypeStruct((1, keep), jnp.int32),
        ),
        compiler_params=params(24),
        cost_estimate=cost(8 * keep * near.size, 4 * near.size + 10 * keep * width),
        name="dispatch_rows",
    )(me, mixed, near, far, rows, gain, label)


def expert_kernel(slots_ref, w_in_ref, w_back_ref, out_ref, entry, hidden, total):
    count, half = slots_ref.shape
    pairs = count // 16
    low_side = iota((pairs, 8, half), 1) < SLOTS
    got = slots_ref[...].astype(jnp.float32).reshape(pairs, 2, 8, half)
    even, odd = got[:, 0], got[:, 1]
    low = jnp.where(low_side, even, pltpu.roll(odd, SLOTS, 1))
    high = jnp.where(low_side, pltpu.roll(even, SLOTS, 1), odd)
    entry[:, :half] = low.reshape(count // 2, half).astype(jnp.bfloat16)
    entry[:, half:] = high.reshape(count // 2, half).astype(jnp.bfloat16)
    tile = 256
    for at in range(0, hidden.shape[1], tile):
        part = dot32(entry[...], w_in_ref[:, at : at + tile])
        hidden[:, at : at + tile] = jnp.maximum(part, 0.0).astype(jnp.bfloat16)
    for at in range(0, total.shape[1], tile):
        total[:, at : at + tile] = dot32(hidden[...], w_back_ref[:, at : at + tile])
    low = total[:, :half].reshape(pairs, 8, half)
    high = total[:, half:].reshape(pairs, 8, half)
    even = jnp.where(low_side, low, pltpu.roll(high, SLOTS, 1))
    odd = jnp.where(low_side, pltpu.roll(low, SLOTS, 1), high)
    both = jnp.concatenate([even[:, None], odd[:, None]], axis=1)
    out_ref[...] = both.reshape(count, half).astype(jnp.bfloat16)


def run_expert(slots, w_in, w_back):
    count, half = slots.shape
    width, inner = w_in.shape
    vmem = pl.BlockSpec(memory_space=pltpu.VMEM)
    return pl.pallas_call(
        expert_kernel,
        in_specs=[vmem] * 3,
        out_specs=vmem,
        out_shape=jax.ShapeDtypeStruct((count, half), jnp.bfloat16),
        scratch_shapes=[
            pltpu.VMEM((count // 2, width), jnp.bfloat16),
            pltpu.VMEM((count // 2, inner), jnp.bfloat16),
            pltpu.VMEM((count // 2, width), jnp.float32),
        ],
        compiler_params=params(16),
        cost_estimate=cost(2 * count * w_in.size, 4 * w_in.size + 4 * slots.size),
        name="run_expert",
    )(slots, w_in, w_back)


def combine_kernel(back_ref, place_ref, first_ref, kept_ref, doc_ref, out_ref):
    back = back_ref[...]
    places, half = back.shape
    place = place_ref[...]
    keep = place.shape[1]
    row = iota((places, keep), 0)
    low = dot_first(one_hot(row == place), back)
    high = dot_first(one_hot(row == place + SLOTS), back)
    taken = jnp.concatenate([low, high], axis=1)
    second = (first_ref[...] + taken).astype(jnp.bfloat16)
    length = doc_ref.shape[0]
    spread = iota((length, keep), 0) == kept_ref[...] % length
    fresh = dot32(one_hot(spread), second).astype(jnp.bfloat16)
    hit = jnp.max(jnp.where(spread, 1.0, 0.0), axis=1, keepdims=True) > 0.5
    out_ref[...] = jnp.where(hit, fresh, doc_ref[...])


def combine(back, place, first, kept, document):
    keep, width = first.shape
    return pl.pallas_call(
        combine_kernel,
        out_shape=jax.ShapeDtypeStruct(document.shape, document.dtype),
        compiler_params=params(16),
        cost_estimate=cost(2 * keep * (2 * back.size + document.size), 6 * document.size),
        name="combine_rows",
    )(back, place, first, kept, document)


def body(
    tokens, kept, gain_attn, gain_ffn, w_query, w_key, w_value, w_out, expert_ids, w_in, w_back
):
    document = tokens[0]
    width = document.shape[1]
    ctx_count = lax.axis_size("ctx")
    experts = lax.axis_size("dp") * ctx_count
    me = lax.axis_index("ctx").astype(jnp.int32)[None]
    keep = kept.shape[1]

    def along(value, step):
        pairs = [(i, (i // 4 + step) % 4 * 4 + i % 4) for i in range(ctx_count)]
        return lax.ppermute(value, "ctx", pairs)

    def flip(value, bit):
        return lax.ppermute(value, "ctx", [(i, i ^ bit) for i in range(ctx_count)])

    heads = (w_query.T, w_key.T, w_value.T)
    rows, normed, own_w = gather_rows(kept, document, gain_attn[None], heads)

    a3, a1, b0 = along(normed, 1), along(normed, 3), flip(normed, 2)
    other_w = flip(own_w, 1)

    def trade(blocks):
        mine, theirs = project(blocks, own_w, other_w)
        return mine, flip(theirs, 1)

    own0, other0 = trade([normed])
    a3, a1, b0, w_mine, own0 = lax.optimization_barrier((a3, a1, b0, w_out, own0))
    low, high, left = (0, 0, HALF), (0, HALF, HALF), (1, HALF, HALF)
    p1, p2, p3 = rearrange([a3, a1, b0], [(low, (2, 0, HALF)), (left, (2, 0, HALF)), (left, high)])
    a3, a1, b0, p1, p2, p3 = lax.optimization_barrier((a3, a1, b0, p1, p2, p3))
    r1, r2, r3 = along(p1, 1), along(p2, 3), flip(p3, 2)
    w_next = lax.ppermute(w_mine, ("dp", "ctx"), [(i, i ^ 18) for i in range(experts)])
    own1, other1 = trade([a3, a1, b0])
    state, *store = attend([own0, own1, other0, other1], [], None, (1024,))
    r1, r2, r3, w_next, state = lax.optimization_barrier((r1, r2, r3, w_next, state))
    count = w_out.shape[0]
    q1, q2, q3, w_pair = rearrange(
        [r1, r2, r3, w_mine, w_next],
        [
            ((0, HALF, THIRD),),
            ((0, THIRD, HALF - THIRD), (1, 0, REST - HALF)),
            ((2, REST - HALF, keep - REST),),
            ((3, 0, count), (4, 0, count)),
        ],
    )
    r1, r2, r3, q1, q2, q3 = lax.optimization_barrier((r1, r2, r3, q1, q2, q3))
    t1, t2, t3 = along(q1, 1), flip(q2, 2), along(q3, 3)
    own2, other2 = trade([r1, r2, r3])
    t1, t2, t3, w_pair, own2 = lax.optimization_barrier((t1, t2, t3, w_pair, own2))
    own3, other3 = trade([t1, t2, t3])
    w_steps = [along(w_pair, 3), along(w_pair, 2), along(w_pair, 1)]
    mixed = attend([own2, own3, other2, other3], [store], state, (1024, 1024), me, ctx_count)
    *w_steps, mixed = lax.optimization_barrier((*w_steps, mixed))
    (w_near,) = rearrange([w_pair, *w_steps], [tuple((k, 0, 2 * count) for k in range(4))])
    w_far = flip(w_near, 1)
    parts = lax.all_to_all(mixed, "ctx", split_axis=0, concat_axis=0, tiled=True)

    label = expert_ids[:, :, 0]
    first, send, place = dispatch(
        me, parts, w_near, w_far, rows, gain_ffn[None], label, experts
    )
    names = ("dp", "ctx")
    send = send.reshape(experts, 2 * SLOTS, width // 2)
    got = lax.all_to_all(send, names, split_axis=0, concat_axis=0, tiled=True)
    answer = run_expert(got.reshape(-1, width // 2), w_in[0], w_back[0])
    answer = answer.reshape(experts, 2 * SLOTS, width // 2)
    back = lax.all_to_all(answer, names, split_axis=0, concat_axis=0, tiled=True)
    return combine(back.reshape(-1, width // 2), place, first, kept, document)[None]


def solution(mesh):
    return jax.shard_map(
        body,
        mesh=mesh,
        in_specs=(
            P("dp", "ctx", None),
            P("dp", "ctx"),
            P(),
            P(),
            P(None, "ctx"),
            P(None, "ctx"),
            P(None, "ctx"),
            P("ctx", None),
            P("dp", "ctx", None),
            P(("dp", "ctx"), None, None),
            P(("dp", "ctx"), None, None),
        ),
        out_specs=P("dp", "ctx", None),
        check_vma=False,
    )
```

```python
import functools
import math

import jax
import jax.numpy as jnp
from jax import lax
from jax.experimental import pallas as pl
from jax.experimental.pallas import tpu as pltpu
from jax.sharding import PartitionSpec as P

HS = 64
LANES = 128
HALF = 128
SLOTS = 4
eps_norm = 1e-06
score_gain = 2.5
SCALE2 = score_gain / math.sqrt(HS) * math.log2(math.e)

A0, A1, A2, A3 = (0, 0), (1, 0), (2, 0), (3, 0)
B0, B1, B2, B3 = (0, 1), (1, 1), (2, 1), (3, 1)
EARLY = [(c, h) for c in (A0, A3, A1, B0) for h in (0, 1)]
LATE = [(A2, 0), (B3, 0), (A2, 1), (B1, 0), (B1, 1), (B3, 1), (B2, 0), (B2, 1)]
THIRD, REST = 48, 208


def params(limit):
    return pltpu.CompilerParams(vmem_limit_bytes=int(limit * 2**20))


def cost(flops, moved, exps=0):
    return pl.CostEstimate(flops=int(flops), bytes_accessed=int(moved), transcendentals=int(exps))


def dot32(a, b):
    return jnp.dot(a, b, preferred_element_type=jnp.float32)


def dot_first(a, b):
    return lax.dot_general(a, b, (((0,), (0,)), ((), ())), preferred_element_type=jnp.float32)


def iota(shape, axis):
    return lax.broadcasted_iota(jnp.int32, shape, axis)


def one_hot(flag):
    return jnp.where(flag, 1.0, 0.0).astype(jnp.bfloat16)


def rms_scale(values, gain):
    power = jnp.mean(values * values, axis=-1, keepdims=True)
    return values * lax.rsqrt(power + eps_norm) * gain


def gather_kernel(*refs):
    sources, (rows_hbm, normed_ref, w_ref, out_ref), (kept, doc, gain, rows_ref, sems) = refs[:7], refs[7:11], refs[11:]
    head = sources[3].shape[0]
    targets = [kept, doc, gain] + [w_ref.at[k * head : (k + 1) * head, :] for k in range(3)] + [out_ref]
    arrivals = [
        pltpu.make_async_copy(source, target, sems.at[k])
        for k, (source, target) in enumerate(zip(sources, targets))
    ]
    for arrival in arrivals:
        arrival.start()
    w_ref[3 * head :, :] = jnp.zeros((w_ref.shape[0] - 3 * head, w_ref.shape[1]), jnp.bfloat16)
    for arrival in arrivals:
        arrival.wait()
    length = doc.shape[0]
    spread = one_hot(iota((length, kept.shape[1]), 0) == kept[...] % length)
    rows = dot_first(spread, doc[...])
    rows_ref[...] = rows.astype(jnp.bfloat16)
    leaving = pltpu.make_async_copy(rows_ref, rows_hbm, sems.at[7])
    leaving.start()
    normed_ref[...] = rms_scale(rows, gain[...]).astype(jnp.bfloat16)
    leaving.wait()


def gather_rows(kept, document, gain, heads):
    keep, (_, width) = kept.shape[1], document.shape
    shape = jax.ShapeDtypeStruct((keep, width), jnp.bfloat16)
    vmem, hbm = pl.BlockSpec(memory_space=pltpu.VMEM), pl.BlockSpec(memory_space=pltpu.HBM)
    return pl.pallas_call(
        gather_kernel,
        in_specs=[hbm] * 7,
        out_specs=[hbm, vmem, vmem, vmem],
        out_shape=(
            shape,
            pltpu.VMEM(shape.shape, jnp.bfloat16),
            pltpu.VMEM((4 * HS, width), jnp.bfloat16),
            pltpu.VMEM(heads[3].shape, jnp.bfloat16),
        ),
        scratch_shapes=[
            pltpu.VMEM(kept.shape, jnp.int32),
            pltpu.VMEM(document.shape, jnp.bfloat16),
            pltpu.VMEM(gain.shape, jnp.float32),
            pltpu.VMEM(shape.shape, jnp.bfloat16),
            pltpu.SemaphoreType.DMA((8,)),
        ],
        compiler_params=params(62.5),
        cost_estimate=cost(2 * keep * document.size, 2 * (document.size + 2 * keep * width)),
        name="gather_rows",
    )(kept, document, gain, *heads)


def rearrange_kernel(*refs, recipes):
    sources, outs = refs[: len(refs) - len(recipes)], refs[len(refs) - len(recipes) :]
    for out, recipe in zip(outs, recipes):
        at = 0
        for which, start, size in recipe:
            out[at : at + size, :] = sources[which][start : start + size, :]
            at += size


def rearrange(sources, recipes):
    width = sources[0].shape[1]
    rows = [sum(size for _, _, size in recipe) for recipe in recipes]
    return pl.pallas_call(
        functools.partial(rearrange_kernel, recipes=recipes),
        out_shape=[jax.ShapeDtypeStruct((count, width), jnp.bfloat16) for count in rows],
        compiler_params=params(8),
        cost_estimate=cost(0, 4 * sum(rows) * width),
        name="rearrange_rows",
    )(*sources)


def dot_last(a, b):
    return lax.dot_general(a, b, (((1,), (1,)), ((), ())), preferred_element_type=jnp.float32)


def project_kernel(*refs):
    *blocks, own_w, other_w, own_ref, other_ref = refs
    at = 0
    for block in blocks:
        here = pl.ds(at, block.shape[0])
        value = block[...]
        own_ref[here, :] = dot_last(value, own_w[...]).astype(jnp.bfloat16)
        other_ref[here, :] = dot_last(value, other_w[...]).astype(jnp.bfloat16)
        at += block.shape[0]


def project(blocks, own_w, other_w):
    count = sum(block.shape[0] for block in blocks)
    columns = own_w.shape[0]
    shape = jax.ShapeDtypeStruct((count, columns), jnp.bfloat16)
    return pl.pallas_call(
        project_kernel,
        out_shape=(shape, shape),
        compiler_params=params(8),
        cost_estimate=cost(1, 1),
        name="project_rows",
    )(*blocks, own_w, other_w)


def unpack(packed, queries, keys, values):
    at = 0
    for piece in packed:
        count = piece.shape[0]
        here = pl.ds(at, count)
        pair = piece[:, :LANES].astype(jnp.float32)
        lane = iota((count, LANES), 1)
        twice = jnp.where(lane < HS, pair, pltpu.roll(pair, HS, 1)) * SCALE2
        high = twice.astype(jnp.bfloat16).astype(jnp.float32)
        queries[here, :] = jnp.where(lane < HS, high, twice - high).astype(jnp.bfloat16)
        turned = pair.T[HS:, :].astype(jnp.bfloat16)
        keys[:HS, here] = turned
        keys[HS:, here] = turned
        ones = jnp.where(lane == HS, 1.0, 0.0)
        values[here, :] = (piece[:, LANES:].astype(jnp.float32) + ones).astype(jnp.bfloat16)
        at += count


def chunks(total, size):
    return [(at, min(size, total - at)) for at in range(0, total, size)]


def online(query, top, held, stores, chunk):
    for keys, values in stores:
        for at, size in chunks(values.shape[0], chunk):
            scores = dot32(query, keys[:, at : at + size])
            newer = jnp.maximum(top, jnp.max(scores, axis=1, keepdims=True))
            weights = jnp.exp2(scores - newer).astype(jnp.bfloat16)
            held = held * jnp.exp2(top - newer) + dot32(weights, values[at : at + size, :])
            top = newer
    return top, held


def block_of(me, chip, side):
    dx, dy = chip
    x, y = me // 4, me // 2 % 2
    return (x + dx) % 4 * 4 + (1 - y if dy else y) * 2 + side


def attend_kernel(*refs, pieces, olds, last, spans):
    refs = list(refs)
    me = refs.pop(0)[0] if last else None
    packed, refs = refs[:pieces], refs[pieces:]
    stores = []
    for _ in range(olds):
        stores.append(refs[:3])
        refs = refs[3:]
    state = refs.pop(0) if olds else None
    out = refs.pop(0)
    queries, keys, values = refs[:3]
    turn = refs[3] if last else None
    unpack(packed, queries, keys, values)

    def finish(side, at, top, held, units):
        size = held.shape[0]
        if not last:
            lane = iota(held.shape, 1)
            out[pl.ds(at, size), :] = jnp.where(lane == HS + 1, top, held)
            return
        turned = held.T
        result = (turned[:HS] / turned[HS : HS + 1]).astype(jnp.bfloat16)
        core = me % 2
        side = jnp.where(side == 0, core, 1 - core)
        for k, (chip, half) in enumerate(units):
            out[block_of(me, chip, side), :, half * HALF : (half + 1) * HALF] = result[
                :, k * HALF : (k + 1) * HALF
            ]

    def each(total, size, step):
        def one(i, carry):
            step(i, pl.multiple_of(i * size, size))
            return carry

        lax.fori_loop(0, total // size, one, 0)

    for old_queries, _, _ in stores:

        def old_step(i, at):
            size = spans[0]
            held = state[pl.ds(at, size), :]
            query = old_queries[pl.ds(at, size), :]
            top = held[:, HS + 1 : HS + 2]
            finish(i, at, *online(query, top, held, [(keys, values)], 1024), EARLY)

        each(old_queries.shape[0], spans[0], old_step)
    seen = [(k, v) for _, k, v in stores] + [(keys, values)]

    def new_step(i, at):
        size = spans[-1]
        top = jnp.full((size, 1), -1e30, jnp.float32)
        held = jnp.zeros((size, LANES), jnp.float32)
        finish(i, at, *online(queries[pl.ds(at, size), :], top, held, seen, 1024), LATE)

    each(queries.shape[0], spans[-1], new_step)


def attend(packed, stores, state, spans, me=None, blocks=0):
    fresh = sum(piece.shape[0] for piece in packed)
    old = sum(store[0].shape[0] for store in stores)
    last = me is not None
    total = old + fresh
    kept_shapes = [(fresh, LANES), (LANES, fresh), (fresh, LANES)]
    vmem = pl.BlockSpec(memory_space=pltpu.VMEM)
    operands = list(packed) + [value for store in stores for value in store]
    operands += [state] if stores else []
    in_specs = [vmem] * len(operands)
    if last:
        operands, in_specs = [me] + operands, [pl.BlockSpec(memory_space=pltpu.SMEM)] + in_specs
        out_shape = jax.ShapeDtypeStruct((blocks, HS, 2 * HALF), jnp.bfloat16)
        scratch = [pltpu.VMEM(shape, jnp.bfloat16) for shape in kept_shapes]
        scratch.append(pltpu.VMEM((LANES, max(spans)), jnp.float32))
        out_specs = vmem
    else:
        out_shape = [jax.ShapeDtypeStruct((old + fresh, LANES), jnp.float32)]
        out_shape += [jax.ShapeDtypeStruct(shape, jnp.bfloat16) for shape in kept_shapes]
        scratch = []
        out_specs = [vmem] * 4
    return pl.pallas_call(
        functools.partial(
            attend_kernel,
            pieces=len(packed),
            olds=len(stores),
            last=last,
            spans=spans,
        ),
        in_specs=in_specs,
        out_specs=out_specs,
        out_shape=out_shape,
        scratch_shapes=scratch,
        compiler_params=params(24),
        cost_estimate=cost(32 * total * total * LANES, 16 * total * LANES) if last else cost(1, 1),
        name="attend_heads",
    )(*operands)


def dispatch_kernel(
    me_ref, mixed_ref, near_ref, far_ref, rows_ref, gain_ref, label_ref, first_ref, send_ref, place_ref, mixed
):
    blocks, head, _ = mixed_ref.shape
    me = me_ref[0]
    x, y = me // 4, me // 2 % 2
    other = jnp.where(x % 2 == 0, x + 1, x - 1)
    columns = (x, other, 3 - x, 3 - other)
    for k in range(blocks):
        side = me % 2 if k < blocks // 2 else 1 - me % 2
        block = columns[k // 2 % 4] * 4 + (1 - y if k % 2 else y) * 2 + side
        mixed[k * head : (k + 1) * head, :] = mixed_ref[block]
    inner = near_ref.shape[0]
    first = dot_first(mixed[:inner, :], near_ref[...]) + dot_first(mixed[inner:, :], far_ref[...])
    first = rows_ref[...].astype(jnp.float32) + first
    first_ref[...] = first
    entry = rms_scale(first, gain_ref[...]).astype(jnp.bfloat16)
    keep, width = first.shape
    label = label_ref[...].astype(jnp.float32)
    across = jnp.broadcast_to(label, (keep, keep))
    same = (across == across.T) & (iota((keep, keep), 0) < iota((keep, keep), 1))
    slot = jnp.sum(jnp.where(same, 1.0, 0.0), axis=0, keepdims=True)
    place = (label * (2 * SLOTS) + slot).astype(jnp.int32)
    place_ref[...] = place
    places = send_ref.shape[0]
    half = width // 2
    row = iota((places, keep), 0)
    send = dot32(one_hot(row == place), entry[:, :half])
    send = send + dot32(one_hot(row == place + SLOTS), entry[:, half:])
    send_ref[...] = send.astype(jnp.bfloat16)


def dispatch(me, mixed, near, far, rows, gain, label, experts):
    keep, width = rows.shape
    places = experts * 2 * SLOTS
    vmem = pl.BlockSpec(memory_space=pltpu.VMEM)
    return pl.pallas_call(
        dispatch_kernel,
        in_specs=[pl.BlockSpec(memory_space=pltpu.SMEM)] + [vmem] * 6,
        scratch_shapes=[pltpu.VMEM((mixed.shape[0] * mixed.shape[1], keep), jnp.bfloat16)],
        out_shape=(
            jax.ShapeDtypeStruct((keep, width), jnp.float32),
            jax.ShapeDtypeStruct((places, width // 2), jnp.bfloat16),
            jax.ShapeDtypeStruct((1, keep), jnp.int32),
        ),
        compiler_params=params(24),
        cost_estimate=cost(8 * keep * near.size, 4 * near.size + 10 * keep * width),
        name="dispatch_rows",
    )(me, mixed, near, far, rows, gain, label)


def expert_kernel(slots_ref, w_in_ref, w_back_ref, out_ref, entry, hidden, total):
    count, half = slots_ref.shape
    pairs = count // 16
    low_side = iota((pairs, 8, half), 1) < SLOTS
    got = slots_ref[...].astype(jnp.float32).reshape(pairs, 2, 8, half)
    even, odd = got[:, 0], got[:, 1]
    low = jnp.where(low_side, even, pltpu.roll(odd, SLOTS, 1))
    high = jnp.where(low_side, pltpu.roll(even, SLOTS, 1), odd)
    entry[:, :half] = low.reshape(count // 2, half).astype(jnp.bfloat16)
    entry[:, half:] = high.reshape(count // 2, half).astype(jnp.bfloat16)
    tile = 256
    for at in range(0, hidden.shape[1], tile):
        part = dot32(entry[...], w_in_ref[:, at : at + tile])
        hidden[:, at : at + tile] = jnp.maximum(part, 0.0).astype(jnp.bfloat16)
    for at in range(0, total.shape[1], tile):
        total[:, at : at + tile] = dot32(hidden[...], w_back_ref[:, at : at + tile])
    low = total[:, :half].reshape(pairs, 8, half)
    high = total[:, half:].reshape(pairs, 8, half)
    even = jnp.where(low_side, low, pltpu.roll(high, SLOTS, 1))
    odd = jnp.where(low_side, pltpu.roll(low, SLOTS, 1), high)
    both = jnp.concatenate([even[:, None], odd[:, None]], axis=1)
    out_ref[...] = both.reshape(count, half).astype(jnp.bfloat16)


def run_expert(slots, w_in, w_back):
    count, half = slots.shape
    width, inner = w_in.shape
    vmem = pl.BlockSpec(memory_space=pltpu.VMEM)
    return pl.pallas_call(
        expert_kernel,
        in_specs=[vmem] * 3,
        out_specs=vmem,
        out_shape=jax.ShapeDtypeStruct((count, half), jnp.bfloat16),
        scratch_shapes=[
            pltpu.VMEM((count // 2, width), jnp.bfloat16),
            pltpu.VMEM((count // 2, inner), jnp.bfloat16),
            pltpu.VMEM((count // 2, width), jnp.float32),
        ],
        compiler_params=params(16),
        cost_estimate=cost(2 * count * w_in.size, 4 * w_in.size + 4 * slots.size),
        name="run_expert",
    )(slots, w_in, w_back)


def combine_kernel(back_ref, place_ref, first_ref, kept_ref, doc_ref, out_ref):
    back = back_ref[...]
    places, half = back.shape
    place = place_ref[...]
    keep = place.shape[1]
    row = iota((places, keep), 0)
    low = dot_first(one_hot(row == place), back)
    high = dot_first(one_hot(row == place + SLOTS), back)
    taken = jnp.concatenate([low, high], axis=1)
    second = (first_ref[...] + taken).astype(jnp.bfloat16)
    length = doc_ref.shape[0]
    spread = iota((length, keep), 0) == kept_ref[...] % length
    fresh = dot32(one_hot(spread), second).astype(jnp.bfloat16)
    hit = jnp.max(jnp.where(spread, 1.0, 0.0), axis=1, keepdims=True) > 0.5
    out_ref[...] = jnp.where(hit, fresh, doc_ref[...])


def combine(back, place, first, kept, document):
    keep, width = first.shape
    return pl.pallas_call(
        combine_kernel,
        out_shape=jax.ShapeDtypeStruct(document.shape, document.dtype),
        compiler_params=params(16),
        cost_estimate=cost(2 * keep * (2 * back.size + document.size), 6 * document.size),
        name="combine_rows",
    )(back, place, first, kept, document)


def body(
    tokens, kept, gain_attn, gain_ffn, w_query, w_key, w_value, w_out, expert_ids, w_in, w_back
):
    document = tokens[0]
    width = document.shape[1]
    ctx_count = lax.axis_size("ctx")
    experts = lax.axis_size("dp") * ctx_count
    me = lax.axis_index("ctx").astype(jnp.int32)[None]
    keep = kept.shape[1]

    def along(value, step):
        pairs = [(i, (i // 4 + step) % 4 * 4 + i % 4) for i in range(ctx_count)]
        return lax.ppermute(value, "ctx", pairs)

    def flip(value, bit):
        return lax.ppermute(value, "ctx", [(i, i ^ bit) for i in range(ctx_count)])

    heads = (w_query.T, w_key.T, w_value.T, w_out)
    me, kept = lax.optimization_barrier((me, kept))
    rows, normed, own_w, w_mine = gather_rows(kept, document, gain_attn[None], heads)

    a3, a1, b0 = along(normed, 1), along(normed, 3), flip(normed, 2)
    other_w = flip(own_w, 1)

    def trade(blocks):
        mine, theirs = project(blocks, own_w, other_w)
        return mine, flip(theirs, 1)

    own0, other0 = trade([normed])
    w_mine, own0 = lax.optimization_barrier((w_mine, own0))
    w_next = lax.ppermute(w_mine, ("dp", "ctx"), [(i, i ^ 18) for i in range(experts)])
    a3, a1, b0, w_next = lax.optimization_barrier((a3, a1, b0, w_next))
    low, high, left = (0, 0, HALF), (0, HALF, HALF), (1, HALF, HALF)
    count = w_out.shape[0]
    p1, p2, p3, w_pair = rearrange(
        [a3, a1, b0, w_mine, w_next],
        [(low, (2, 0, HALF)), (left, (2, 0, HALF)), (left, high), ((3, 0, count), (4, 0, count))],
    )
    a3, a1, b0, p1, p2, p3 = lax.optimization_barrier((a3, a1, b0, p1, p2, p3))
    r1, r2, r3 = along(p1, 1), along(p2, 3), flip(p3, 2)
    own1, other1 = trade([a3, a1, b0])
    state, *store = attend([own0, own1, other0, other1], [], None, (1024,))
    r1, r2, r3, state = lax.optimization_barrier((r1, r2, r3, state))
    q1, q2, q3 = rearrange(
        [r1, r2, r3],
        [
            ((0, HALF, THIRD),),
            ((0, THIRD, HALF - THIRD), (1, 0, REST - HALF)),
            ((2, REST - HALF, keep - REST),),
        ],
    )
    r1, r2, r3, q1, q2, q3 = lax.optimization_barrier((r1, r2, r3, q1, q2, q3))
    t1, t2, t3 = along(q1, 1), flip(q2, 2), along(q3, 3)
    own2, other2 = trade([r1, r2, r3])
    w_pair, own2 = lax.optimization_barrier((w_pair, own2))
    w_side = lax.ppermute(w_pair, "ctx", [(i, i ^ 4) for i in range(ctx_count)])
    t1, t2, t3, w_side = lax.optimization_barrier((t1, t2, t3, w_side))
    own3, other3 = trade([t1, t2, t3])
    (w_quad,) = rearrange([w_pair, w_side], [((0, 0, 2 * count), (1, 0, 2 * count))])
    w_rest = lax.ppermute(w_quad, "ctx", [(i, i ^ 12) for i in range(ctx_count)])
    mixed = attend([own2, own3, other2, other3], [store], state, (1024, 1024), me, ctx_count)
    w_quad, w_rest, mixed = lax.optimization_barrier((w_quad, w_rest, mixed))
    (w_near,) = rearrange([w_quad, w_rest], [((0, 0, 4 * count), (1, 0, 4 * count))])
    w_far = flip(w_near, 1)
    parts = lax.all_to_all(mixed, "ctx", split_axis=0, concat_axis=0, tiled=True)

    label = expert_ids[:, :, 0]
    first, send, place = dispatch(
        me, parts, w_near, w_far, rows, gain_ffn[None], label, experts
    )
    names = ("dp", "ctx")
    send = send.reshape(experts, 2 * SLOTS, width // 2)
    got = lax.all_to_all(send, names, split_axis=0, concat_axis=0, tiled=True)
    answer = run_expert(got.reshape(-1, width // 2), w_in[0], w_back[0])
    answer = answer.reshape(experts, 2 * SLOTS, width // 2)
    back = lax.all_to_all(answer, names, split_axis=0, concat_axis=0, tiled=True)
    return combine(back.reshape(-1, width // 2), place, first, kept, document)[None]


def solution(mesh):
    return jax.shard_map(
        body,
        mesh=mesh,
        in_specs=(
            P("dp", "ctx", None),
            P("dp", "ctx"),
            P(),
            P(),
            P(None, "ctx"),
            P(None, "ctx"),
            P(None, "ctx"),
            P("ctx", None),
            P("dp", "ctx", None),
            P(("dp", "ctx"), None, None),
            P(("dp", "ctx"), None, None),
        ),
        out_specs=P("dp", "ctx", None),
        check_vma=False,
    )
```

```python
import functools
import math

import jax
import jax.numpy as jnp
from jax import lax
from jax.experimental import pallas as pl
from jax.experimental.pallas import tpu as pltpu
from jax.sharding import PartitionSpec as P

HS = 64
LANES = 128
HALF = 128
SLOTS = 4
eps_norm = 1e-06
score_gain = 2.5
SCALE2 = score_gain / math.sqrt(HS) * math.log2(math.e)

A0, A1, A2, A3 = (0, 0), (1, 0), (2, 0), (3, 0)
B0, B1, B2, B3 = (0, 1), (1, 1), (2, 1), (3, 1)
EARLY = [(c, h) for c in (A0, A3, A1, B0) for h in (0, 1)]
LATE = [(A2, 0), (B3, 0), (A2, 1), (B1, 0), (B1, 1), (B3, 1), (B2, 0), (B2, 1)]
THIRD, REST = 48, 208


def params(limit):
    return pltpu.CompilerParams(vmem_limit_bytes=int(limit * 2**20))


def cost(flops, moved, exps=0):
    return pl.CostEstimate(flops=int(flops), bytes_accessed=int(moved), transcendentals=int(exps))


def dot32(a, b):
    return jnp.dot(a, b, preferred_element_type=jnp.float32)


def dot_first(a, b):
    return lax.dot_general(a, b, (((0,), (0,)), ((), ())), preferred_element_type=jnp.float32)


def iota(shape, axis):
    return lax.broadcasted_iota(jnp.int32, shape, axis)


def one_hot(flag):
    return jnp.where(flag, 1.0, 0.0).astype(jnp.bfloat16)


def rms_scale(values, gain):
    power = jnp.mean(values * values, axis=-1, keepdims=True)
    return values * lax.rsqrt(power + eps_norm) * gain


def gather_kernel(*refs):
    sources, (rows_hbm, normed_ref, w_ref, out_ref), (kept, doc, gain, rows_ref, sems) = refs[:7], refs[7:11], refs[11:]
    head = sources[3].shape[0]
    targets = [kept, doc, gain] + [w_ref.at[k * head : (k + 1) * head, :] for k in range(3)] + [out_ref]
    arrivals = [
        pltpu.make_async_copy(source, target, sems.at[k])
        for k, (source, target) in enumerate(zip(sources, targets))
    ]
    for arrival in arrivals:
        arrival.start()
    w_ref[3 * head :, :] = jnp.zeros((w_ref.shape[0] - 3 * head, w_ref.shape[1]), jnp.bfloat16)
    for arrival in arrivals:
        arrival.wait()
    length = doc.shape[0]
    spread = one_hot(iota((length, kept.shape[1]), 0) == kept[...] % length)
    rows = dot_first(spread, doc[...])
    rows_ref[...] = rows.astype(jnp.bfloat16)
    leaving = pltpu.make_async_copy(rows_ref, rows_hbm, sems.at[7])
    leaving.start()
    normed_ref[...] = rms_scale(rows, gain[...]).astype(jnp.bfloat16)
    leaving.wait()


def gather_rows(kept, document, gain, heads):
    keep, (_, width) = kept.shape[1], document.shape
    shape = jax.ShapeDtypeStruct((keep, width), jnp.bfloat16)
    vmem, hbm = pl.BlockSpec(memory_space=pltpu.VMEM), pl.BlockSpec(memory_space=pltpu.HBM)
    return pl.pallas_call(
        gather_kernel,
        in_specs=[hbm] * 7,
        out_specs=[hbm, vmem, vmem, vmem],
        out_shape=(
            shape,
            pltpu.VMEM(shape.shape, jnp.bfloat16),
            pltpu.VMEM((4 * HS, width), jnp.bfloat16),
            pltpu.VMEM(heads[3].shape, jnp.bfloat16),
        ),
        scratch_shapes=[
            pltpu.VMEM(kept.shape, jnp.int32),
            pltpu.VMEM(document.shape, jnp.bfloat16),
            pltpu.VMEM(gain.shape, jnp.float32),
            pltpu.VMEM(shape.shape, jnp.bfloat16),
            pltpu.SemaphoreType.DMA((8,)),
        ],
        compiler_params=params(62.5),
        cost_estimate=cost(2 * keep * document.size, 2 * (document.size + 2 * keep * width)),
        name="gather_rows",
    )(kept, document, gain, *heads)


def rearrange_kernel(*refs, recipes):
    sources, outs = refs[: len(refs) - len(recipes)], refs[len(refs) - len(recipes) :]
    for out, recipe in zip(outs, recipes):
        at = 0
        for which, start, size in recipe:
            out[at : at + size, :] = sources[which][start : start + size, :]
            at += size


def rearrange(sources, recipes):
    width = sources[0].shape[1]
    rows = [sum(size for _, _, size in recipe) for recipe in recipes]
    return pl.pallas_call(
        functools.partial(rearrange_kernel, recipes=recipes),
        out_shape=[jax.ShapeDtypeStruct((count, width), jnp.bfloat16) for count in rows],
        compiler_params=params(8),
        cost_estimate=cost(0, 4 * sum(rows) * width),
        name="rearrange_rows",
    )(*sources)


def dot_last(a, b):
    return lax.dot_general(a, b, (((1,), (1,)), ((), ())), preferred_element_type=jnp.float32)


def project_kernel(*refs):
    *blocks, own_w, other_w, own_ref, other_ref = refs
    at = 0
    for block in blocks:
        here = pl.ds(at, block.shape[0])
        value = block[...]
        own_ref[here, :] = dot_last(value, own_w[...]).astype(jnp.bfloat16)
        other_ref[here, :] = dot_last(value, other_w[...]).astype(jnp.bfloat16)
        at += block.shape[0]


def project(blocks, own_w, other_w):
    count = sum(block.shape[0] for block in blocks)
    columns = own_w.shape[0]
    shape = jax.ShapeDtypeStruct((count, columns), jnp.bfloat16)
    return pl.pallas_call(
        project_kernel,
        out_shape=(shape, shape),
        compiler_params=params(8),
        cost_estimate=cost(1, 1),
        name="project_rows",
    )(*blocks, own_w, other_w)


def unpack(packed, queries, keys, values):
    at = 0
    for piece in packed:
        count = piece.shape[0]
        here = pl.ds(at, count)
        pair = piece[:, :LANES].astype(jnp.float32)
        lane = iota((count, LANES), 1)
        twice = jnp.where(lane < HS, pair, pltpu.roll(pair, HS, 1)) * SCALE2
        high = twice.astype(jnp.bfloat16).astype(jnp.float32)
        queries[here, :] = jnp.where(lane < HS, high, twice - high).astype(jnp.bfloat16)
        turned = pair.T[HS:, :].astype(jnp.bfloat16)
        keys[:HS, here] = turned
        keys[HS:, here] = turned
        ones = jnp.where(lane == HS, 1.0, 0.0)
        values[here, :] = (piece[:, LANES:].astype(jnp.float32) + ones).astype(jnp.bfloat16)
        at += count


def chunks(total, size):
    size = total if total < 1600 else size
    return [(at, min(size, total - at)) for at in range(0, total, size)]


def online(query, top, held, stores, chunk):
    for keys, values in stores:
        for at, size in chunks(values.shape[0], chunk):
            scores = dot32(query, keys[:, at : at + size])
            newer = jnp.maximum(top, jnp.max(scores, axis=1, keepdims=True))
            weights = jnp.exp2(scores - newer).astype(jnp.bfloat16)
            held = held * jnp.exp2(top - newer) + dot32(weights, values[at : at + size, :])
            top = newer
    return top, held


def block_of(me, chip, side):
    dx, dy = chip
    x, y = me // 4, me // 2 % 2
    return (x + dx) % 4 * 4 + (1 - y if dy else y) * 2 + side


def attend_kernel(*refs, pieces, olds, last, span):
    refs = list(refs)
    me = refs.pop(0)[0] if last else None
    packed, refs = refs[:pieces], refs[pieces:]
    stores = []
    for _ in range(olds):
        stores.append(refs[:3])
        refs = refs[3:]
    state = refs.pop(0) if olds else None
    out = refs.pop(0)
    queries, keys, values = refs[:3]
    unpack(packed, queries, keys, values)

    def finish(side, at, top, held, units):
        if not last:
            lane = iota(held.shape, 1)
            out[pl.ds(at, span), :] = jnp.where(lane == HS + 1, top, held)
            return
        turned = held.T
        result = (turned[:HS] / turned[HS : HS + 1]).astype(jnp.bfloat16)
        core = me % 2
        side = jnp.where(side == 0, core, 1 - core)
        for k, (chip, half) in enumerate(units):
            out[block_of(me, chip, side), :, half * HALF : (half + 1) * HALF] = result[
                :, k * HALF : (k + 1) * HALF
            ]

    def each(total, step):
        def one(i, carry):
            step(i, pl.multiple_of(i * span, span))
            return carry

        if last:
            for i in range(total // span):
                step(i, i * span)
        else:
            lax.fori_loop(0, total // span, one, 0)

    if stores:

        def old_step(i, at):
            held = state[pl.ds(at, span), :]
            query = stores[0][0][pl.ds(at, span), :]
            top = held[:, HS + 1 : HS + 2]
            finish(i, at, *online(query, top, held, [(keys, values)], 1024), EARLY)

        each(stores[0][0].shape[0], old_step)
    if last:
        late, at = refs[3], 0
        for side in range(2):
            for source in (stores[1][0], queries):
                count = source.shape[0] // 2
                late[at : at + count, :] = source[side * count : (side + 1) * count, :]
                at += count
    if last or not stores:
        seen = [(k, v) for _, k, v in stores] + [(keys, values)]
        fresh = late if last else queries

        def new_step(i, at):
            top = jnp.full((span, 1), -1e30, jnp.float32)
            held = jnp.zeros((span, LANES), jnp.float32)
            finish(i, at, *online(fresh[pl.ds(at, span), :], top, held, seen, 1024), LATE)

        each(fresh.shape[0], new_step)


def attend(packed, stores=(), state=None, me=None, blocks=0):
    fresh = sum(piece.shape[0] for piece in packed)
    old = sum(store[0].shape[0] for store in stores)
    last = me is not None
    total = old + fresh
    span = 1024
    kept_shapes = [(fresh, LANES), (LANES, fresh), (fresh, LANES)]
    vmem = pl.BlockSpec(memory_space=pltpu.VMEM)
    operands = list(packed) + [value for store in stores for value in store]
    operands += [state] if stores else []
    in_specs = [vmem] * len(operands)
    if last:
        operands, in_specs = [me] + operands, [pl.BlockSpec(memory_space=pltpu.SMEM)] + in_specs
        out_shape = jax.ShapeDtypeStruct((blocks, HS, 2 * HALF), jnp.bfloat16)
        scratch = [pltpu.VMEM(shape, jnp.bfloat16) for shape in kept_shapes]
        scratch.append(pltpu.VMEM((total - stores[0][0].shape[0], LANES), jnp.bfloat16))
        out_specs = vmem
    else:
        out_shape = [jax.ShapeDtypeStruct((old if stores else fresh, LANES), jnp.float32)]
        out_shape += [jax.ShapeDtypeStruct(shape, jnp.bfloat16) for shape in kept_shapes]
        scratch = []
        out_specs = [vmem] * 4
    return pl.pallas_call(
        functools.partial(
            attend_kernel, pieces=len(packed), olds=len(stores), last=last, span=span
        ),
        in_specs=in_specs,
        out_specs=out_specs,
        out_shape=out_shape,
        scratch_shapes=scratch,
        compiler_params=params(24),
        cost_estimate=cost(32 * total * total * LANES, 16 * total * LANES) if last else cost(1, 1),
        name="attend_heads",
    )(*operands)


def dispatch_kernel(
    me_ref, mixed_ref, near_ref, far_ref, rows_ref, gain_ref, label_ref, first_ref, send_ref, place_ref, mixed
):
    blocks, head, _ = mixed_ref.shape
    me = me_ref[0]
    x, y = me // 4, me // 2 % 2
    other = jnp.where(x % 2 == 0, x + 1, x - 1)
    columns = (x, other, 3 - x, 3 - other)
    for k in range(blocks):
        side = me % 2 if k < blocks // 2 else 1 - me % 2
        block = columns[k // 2 % 4] * 4 + (1 - y if k % 2 else y) * 2 + side
        mixed[k * head : (k + 1) * head, :] = mixed_ref[block]
    inner = near_ref.shape[0]
    first = dot_first(mixed[:inner, :], near_ref[...]) + dot_first(mixed[inner:, :], far_ref[...])
    first = rows_ref[...].astype(jnp.float32) + first
    first_ref[...] = first
    entry = rms_scale(first, gain_ref[...]).astype(jnp.bfloat16)
    keep, width = first.shape
    label = label_ref[...].astype(jnp.float32)
    across = jnp.broadcast_to(label, (keep, keep))
    same = (across == across.T) & (iota((keep, keep), 0) < iota((keep, keep), 1))
    slot = jnp.sum(jnp.where(same, 1.0, 0.0), axis=0, keepdims=True)
    place = (label * (2 * SLOTS) + slot).astype(jnp.int32)
    place_ref[...] = place
    places = send_ref.shape[0]
    half = width // 2
    row = iota((places, keep), 0)
    send = dot32(one_hot(row == place), entry[:, :half])
    send = send + dot32(one_hot(row == place + SLOTS), entry[:, half:])
    send_ref[...] = send.astype(jnp.bfloat16)


def dispatch(me, mixed, near, far, rows, gain, label, experts):
    keep, width = rows.shape
    places = experts * 2 * SLOTS
    vmem = pl.BlockSpec(memory_space=pltpu.VMEM)
    return pl.pallas_call(
        dispatch_kernel,
        in_specs=[pl.BlockSpec(memory_space=pltpu.SMEM)] + [vmem] * 6,
        scratch_shapes=[pltpu.VMEM((mixed.shape[0] * mixed.shape[1], keep), jnp.bfloat16)],
        out_shape=(
            jax.ShapeDtypeStruct((keep, width), jnp.float32),
            jax.ShapeDtypeStruct((places, width // 2), jnp.bfloat16),
            jax.ShapeDtypeStruct((1, keep), jnp.int32),
        ),
        compiler_params=params(24),
        cost_estimate=cost(8 * keep * near.size, 4 * near.size + 10 * keep * width),
        name="dispatch_rows",
    )(me, mixed, near, far, rows, gain, label)


def expert_kernel(slots_ref, w_in_ref, w_back_ref, out_ref, entry, hidden, total):
    count, half = slots_ref.shape
    pairs = count // 16
    low_side = iota((pairs, 8, half), 1) < SLOTS
    got = slots_ref[...].astype(jnp.float32).reshape(pairs, 2, 8, half)
    even, odd = got[:, 0], got[:, 1]
    low = jnp.where(low_side, even, pltpu.roll(odd, SLOTS, 1))
    high = jnp.where(low_side, pltpu.roll(even, SLOTS, 1), odd)
    entry[:, :half] = low.reshape(count // 2, half).astype(jnp.bfloat16)
    entry[:, half:] = high.reshape(count // 2, half).astype(jnp.bfloat16)
    tile = 256
    for at in range(0, hidden.shape[1], tile):
        part = dot32(entry[...], w_in_ref[:, at : at + tile])
        hidden[:, at : at + tile] = jnp.maximum(part, 0.0).astype(jnp.bfloat16)
    for at in range(0, total.shape[1], tile):
        total[:, at : at + tile] = dot32(hidden[...], w_back_ref[:, at : at + tile])
    low = total[:, :half].reshape(pairs, 8, half)
    high = total[:, half:].reshape(pairs, 8, half)
    even = jnp.where(low_side, low, pltpu.roll(high, SLOTS, 1))
    odd = jnp.where(low_side, pltpu.roll(low, SLOTS, 1), high)
    both = jnp.concatenate([even[:, None], odd[:, None]], axis=1)
    out_ref[...] = both.reshape(count, half).astype(jnp.bfloat16)


def run_expert(slots, w_in, w_back):
    count, half = slots.shape
    width, inner = w_in.shape
    vmem = pl.BlockSpec(memory_space=pltpu.VMEM)
    return pl.pallas_call(
        expert_kernel,
        in_specs=[vmem] * 3,
        out_specs=vmem,
        out_shape=jax.ShapeDtypeStruct((count, half), jnp.bfloat16),
        scratch_shapes=[
            pltpu.VMEM((count // 2, width), jnp.bfloat16),
            pltpu.VMEM((count // 2, inner), jnp.bfloat16),
            pltpu.VMEM((count // 2, width), jnp.float32),
        ],
        compiler_params=params(16),
        cost_estimate=cost(2 * count * w_in.size, 4 * w_in.size + 4 * slots.size),
        name="run_expert",
    )(slots, w_in, w_back)


def combine_kernel(back_ref, place_ref, first_ref, kept_ref, doc_ref, out_ref):
    back = back_ref[...]
    places, half = back.shape
    place = place_ref[...]
    keep = place.shape[1]
    row = iota((places, keep), 0)
    low = dot_first(one_hot(row == place), back)
    high = dot_first(one_hot(row == place + SLOTS), back)
    taken = jnp.concatenate([low, high], axis=1)
    second = (first_ref[...] + taken).astype(jnp.bfloat16)
    length = doc_ref.shape[0]
    spread = iota((length, keep), 0) == kept_ref[...] % length
    fresh = dot32(one_hot(spread), second).astype(jnp.bfloat16)
    hit = jnp.max(jnp.where(spread, 1.0, 0.0), axis=1, keepdims=True) > 0.5
    out_ref[...] = jnp.where(hit, fresh, doc_ref[...])


def combine(back, place, first, kept, document):
    keep, width = first.shape
    return pl.pallas_call(
        combine_kernel,
        out_shape=jax.ShapeDtypeStruct(document.shape, document.dtype),
        compiler_params=params(16),
        cost_estimate=cost(2 * keep * (2 * back.size + document.size), 6 * document.size),
        name="combine_rows",
    )(back, place, first, kept, document)


def body(
    tokens, kept, gain_attn, gain_ffn, w_query, w_key, w_value, w_out, expert_ids, w_in, w_back
):
    document = tokens[0]
    width = document.shape[1]
    ctx_count = lax.axis_size("ctx")
    experts = lax.axis_size("dp") * ctx_count
    me = lax.axis_index("ctx").astype(jnp.int32)[None]
    keep = kept.shape[1]

    def along(value, step):
        pairs = [(i, (i // 4 + step) % 4 * 4 + i % 4) for i in range(ctx_count)]
        return lax.ppermute(value, "ctx", pairs)

    def flip(value, bit):
        return lax.ppermute(value, "ctx", [(i, i ^ bit) for i in range(ctx_count)])

    heads = (w_query.T, w_key.T, w_value.T, w_out)
    me, kept = lax.optimization_barrier((me, kept))
    rows, normed, own_w, w_mine = gather_rows(kept, document, gain_attn[None], heads)

    b0, a1, a3 = flip(normed, 2), along(normed, 3), along(normed, 1)
    other_w = flip(own_w, 1)

    def trade(blocks):
        mine, theirs = project(blocks, own_w, other_w)
        return mine, flip(theirs, 1)

    own0, other0 = trade([normed])
    w_mine, own0 = lax.optimization_barrier((w_mine, own0))
    w_next = lax.ppermute(w_mine, ("dp", "ctx"), [(i, i ^ 18) for i in range(experts)])
    a3, a1, b0, w_next = lax.optimization_barrier((a3, a1, b0, w_next))
    low, high, left = (0, 0, HALF), (0, HALF, HALF), (1, HALF, HALF)
    count = w_out.shape[0]
    p1, p2, p3, w_pair = rearrange(
        [a3, a1, b0, w_mine, w_next],
        [(low, (2, 0, HALF)), (left, (2, 0, HALF)), (left, high), ((3, 0, count), (4, 0, count))],
    )
    a3, a1, b0, p1, p2, p3 = lax.optimization_barrier((a3, a1, b0, p1, p2, p3))
    r1, r2, r3 = along(p1, 1), along(p2, 3), flip(p3, 2)
    own1, other1 = trade([a3, a1, b0])
    state, *store = attend([own0, own1, other0, other1])
    r1, r2, r3, state = lax.optimization_barrier((r1, r2, r3, state))
    q1, q2, q3 = rearrange(
        [r1, r2, r3],
        [
            ((0, HALF, THIRD),),
            ((0, THIRD, HALF - THIRD), (1, 0, REST - HALF)),
            ((2, REST - HALF, keep - REST),),
        ],
    )
    r1, r2, r3, q1, q2, q3 = lax.optimization_barrier((r1, r2, r3, q1, q2, q3))
    t1, t2, t3 = along(q1, 1), flip(q2, 2), along(q3, 3)
    own2, other2 = trade([r1, r2, r3])
    w_pair, own2 = lax.optimization_barrier((w_pair, own2))
    w_side = lax.ppermute(w_pair, "ctx", [(i, i ^ 4) for i in range(ctx_count)])
    state, *later = attend([own2, other2], [store], state)
    t1, t2, t3, w_side, state = lax.optimization_barrier((t1, t2, t3, w_side, state))
    own3, other3 = trade([t1, t2, t3])
    (w_quad,) = rearrange([w_pair, w_side], [((0, 0, 2 * count), (1, 0, 2 * count))])
    w_rest = lax.ppermute(w_quad, "ctx", [(i, i ^ 12) for i in range(ctx_count)])
    mixed = attend([own3, other3], [store, later], state, me, ctx_count)
    w_quad, w_rest, mixed = lax.optimization_barrier((w_quad, w_rest, mixed))
    (w_near,) = rearrange([w_quad, w_rest], [((0, 0, 4 * count), (1, 0, 4 * count))])
    w_far = flip(w_near, 1)
    parts = lax.all_to_all(mixed, "ctx", split_axis=0, concat_axis=0, tiled=True)

    label = expert_ids[:, :, 0]
    first, send, place = dispatch(
        me, parts, w_near, w_far, rows, gain_ffn[None], label, experts
    )
    names = ("dp", "ctx")
    send = send.reshape(experts, 2 * SLOTS, width // 2)
    got = lax.all_to_all(send, names, split_axis=0, concat_axis=0, tiled=True)
    answer = run_expert(got.reshape(-1, width // 2), w_in[0], w_back[0])
    answer = answer.reshape(experts, 2 * SLOTS, width // 2)
    back = lax.all_to_all(answer, names, split_axis=0, concat_axis=0, tiled=True)
    return combine(back.reshape(-1, width // 2), place, first, kept, document)[None]


def solution(mesh):
    return jax.shard_map(
        body,
        mesh=mesh,
        in_specs=(
            P("dp", "ctx", None),
            P("dp", "ctx"),
            P(),
            P(),
            P(None, "ctx"),
            P(None, "ctx"),
            P(None, "ctx"),
            P("ctx", None),
            P("dp", "ctx", None),
            P(("dp", "ctx"), None, None),
            P(("dp", "ctx"), None, None),
        ),
        out_specs=P("dp", "ctx", None),
        check_vma=False,
    )
```

```python
import functools
import math

import jax
import jax.numpy as jnp
from jax import lax
from jax.experimental import pallas as pl
from jax.experimental.pallas import tpu as pltpu
from jax.sharding import PartitionSpec as P

HS = 64
LANES = 128
HALF = 128
SLOTS = 4
eps_norm = 1e-06
score_gain = 2.5
SCALE2 = score_gain / math.sqrt(HS) * math.log2(math.e)

A0, A1, A2, A3 = (0, 0), (1, 0), (2, 0), (3, 0)
B0, B1, B2, B3 = (0, 1), (1, 1), (2, 1), (3, 1)
EARLY = [(c, h) for c in (A0, A3, A1, B0) for h in (0, 1)]
LATE = [(A2, 0), (B3, 0), (A2, 1), (B1, 0), (B1, 1), (B3, 1), (B2, 0), (B2, 1)]
PART = 96


def params(limit):
    return pltpu.CompilerParams(vmem_limit_bytes=int(limit * 2**20))


def cost(flops, moved, exps=0):
    return pl.CostEstimate(flops=int(flops), bytes_accessed=int(moved), transcendentals=int(exps))


def dot32(a, b):
    return jnp.dot(a, b, preferred_element_type=jnp.float32)


def dot_first(a, b):
    return lax.dot_general(a, b, (((0,), (0,)), ((), ())), preferred_element_type=jnp.float32)


def iota(shape, axis):
    return lax.broadcasted_iota(jnp.int32, shape, axis)


def one_hot(flag):
    return jnp.where(flag, 1.0, 0.0).astype(jnp.bfloat16)


def rms_scale(values, gain):
    power = jnp.mean(values * values, axis=-1, keepdims=True)
    return values * lax.rsqrt(power + eps_norm) * gain


def gather_kernel(*refs):
    sources, (rows_hbm, normed_ref, w_ref, out_ref), (kept, doc, gain, rows_ref, sems) = refs[:7], refs[7:11], refs[11:]
    head = sources[3].shape[0]
    targets = [kept, doc, gain] + [w_ref.at[k * head : (k + 1) * head, :] for k in range(3)] + [out_ref]
    arrivals = [
        pltpu.make_async_copy(source, target, sems.at[k])
        for k, (source, target) in enumerate(zip(sources, targets))
    ]
    for arrival in arrivals:
        arrival.start()
    w_ref[3 * head :, :] = jnp.zeros((w_ref.shape[0] - 3 * head, w_ref.shape[1]), jnp.bfloat16)
    for arrival in arrivals:
        arrival.wait()
    length = doc.shape[0]
    spread = one_hot(iota((length, kept.shape[1]), 0) == kept[...] % length)
    rows = dot_first(spread, doc[...])
    rows_ref[...] = rows.astype(jnp.bfloat16)
    leaving = pltpu.make_async_copy(rows_ref, rows_hbm, sems.at[7])
    leaving.start()
    normed_ref[...] = rms_scale(rows, gain[...]).astype(jnp.bfloat16)
    leaving.wait()


def gather_rows(kept, document, gain, heads):
    keep, (_, width) = kept.shape[1], document.shape
    shape = jax.ShapeDtypeStruct((keep, width), jnp.bfloat16)
    vmem, hbm = pl.BlockSpec(memory_space=pltpu.VMEM), pl.BlockSpec(memory_space=pltpu.HBM)
    return pl.pallas_call(
        gather_kernel,
        in_specs=[hbm] * 7,
        out_specs=[hbm, vmem, vmem, vmem],
        out_shape=(
            shape,
            pltpu.VMEM(shape.shape, jnp.bfloat16),
            pltpu.VMEM((4 * HS, width), jnp.bfloat16),
            pltpu.VMEM(heads[3].shape, jnp.bfloat16),
        ),
        scratch_shapes=[
            pltpu.VMEM(kept.shape, jnp.int32),
            pltpu.VMEM(document.shape, jnp.bfloat16),
            pltpu.VMEM(gain.shape, jnp.float32),
            pltpu.VMEM(shape.shape, jnp.bfloat16),
            pltpu.SemaphoreType.DMA((8,)),
        ],
        compiler_params=params(62.5),
        cost_estimate=cost(2 * keep * document.size, 2 * (document.size + 2 * keep * width)),
        name="gather_rows",
    )(kept, document, gain, *heads)


def rearrange_kernel(*refs, recipes):
    sources, outs = refs[: len(refs) - len(recipes)], refs[len(refs) - len(recipes) :]
    for out, recipe in zip(outs, recipes):
        at = 0
        for which, start, size in recipe:
            out[at : at + size, :] = sources[which][start : start + size, :]
            at += size


def rearrange(sources, recipes):
    width = sources[0].shape[1]
    rows = [sum(size for _, _, size in recipe) for recipe in recipes]
    return pl.pallas_call(
        functools.partial(rearrange_kernel, recipes=recipes),
        out_shape=[jax.ShapeDtypeStruct((count, width), jnp.bfloat16) for count in rows],
        compiler_params=params(8),
        cost_estimate=cost(0, 4 * sum(rows) * width),
        name="rearrange_rows",
    )(*sources)


def dot_last(a, b):
    return lax.dot_general(a, b, (((1,), (1,)), ((), ())), preferred_element_type=jnp.float32)


def project_kernel(*refs):
    *blocks, own_w, other_w, own_ref, other_ref = refs
    at = 0
    for block in blocks:
        here = pl.ds(at, block.shape[0])
        value = block[...]
        own_ref[here, :] = dot_last(value, own_w[...]).astype(jnp.bfloat16)
        other_ref[here, :] = dot_last(value, other_w[...]).astype(jnp.bfloat16)
        at += block.shape[0]


def project(blocks, own_w, other_w):
    count = sum(block.shape[0] for block in blocks)
    columns = own_w.shape[0]
    shape = jax.ShapeDtypeStruct((count, columns), jnp.bfloat16)
    return pl.pallas_call(
        project_kernel,
        out_shape=(shape, shape),
        compiler_params=params(8),
        cost_estimate=cost(1, 1),
        name="project_rows",
    )(*blocks, own_w, other_w)


def unpack(packed, queries, keys, values):
    at = 0
    for piece in packed:
        count = piece.shape[0]
        here = pl.ds(at, count)
        pair = piece[:, :LANES].astype(jnp.float32)
        lane = iota((count, LANES), 1)
        twice = jnp.where(lane < HS, pair, pltpu.roll(pair, HS, 1)) * SCALE2
        high = twice.astype(jnp.bfloat16).astype(jnp.float32)
        queries[here, :] = jnp.where(lane < HS, high, twice - high).astype(jnp.bfloat16)
        turned = pair.T[HS:, :].astype(jnp.bfloat16)
        keys[:HS, here] = turned
        keys[HS:, here] = turned
        ones = jnp.where(lane == HS, 1.0, 0.0)
        values[here, :] = (piece[:, LANES:].astype(jnp.float32) + ones).astype(jnp.bfloat16)
        at += count


def chunks(total, size):
    size = total if total < 1600 else size
    return [(at, min(size, total - at)) for at in range(0, total, size)]


def online(query, top, held, stores, chunk):
    for keys, values in stores:
        for at, size in chunks(values.shape[0], chunk):
            scores = dot32(query, keys[:, at : at + size])
            newer = jnp.maximum(top, jnp.max(scores, axis=1, keepdims=True))
            weights = jnp.exp2(scores - newer).astype(jnp.bfloat16)
            held = held * jnp.exp2(top - newer) + dot32(weights, values[at : at + size, :])
            top = newer
    return top, held


def block_of(me, chip, side):
    dx, dy = chip
    x, y = me // 4, me // 2 % 2
    return (x + dx) % 4 * 4 + (1 - y if dy else y) * 2 + side


def attend_kernel(*refs, pieces, olds, last, span):
    refs = list(refs)
    me = refs.pop(0)[0] if last else None
    packed, refs = refs[:pieces], refs[pieces:]
    stores = []
    for _ in range(olds):
        stores.append(refs[:3])
        refs = refs[3:]
    state = refs.pop(0) if olds else None
    out = refs.pop(0)
    queries, keys, values = refs[:3]
    unpack(packed, queries, keys, values)

    def finish(side, at, top, held, units):
        if not last:
            lane = iota(held.shape, 1)
            out[pl.ds(at, span), :] = jnp.where(lane == HS + 1, top, held)
            return
        turned = held.T
        result = (turned[:HS] / turned[HS : HS + 1]).astype(jnp.bfloat16)
        core = me % 2
        side = jnp.where(side == 0, core, 1 - core)
        for k, (chip, half) in enumerate(units):
            out[block_of(me, chip, side), :, half * HALF : (half + 1) * HALF] = result[
                :, k * HALF : (k + 1) * HALF
            ]

    def each(total, step):
        def one(i, carry):
            step(i, pl.multiple_of(i * span, span))
            return carry

        if last:
            for i in range(total // span):
                step(i, i * span)
        else:
            lax.fori_loop(0, total // span, one, 0)

    if stores:

        def old_step(i, at):
            held = state[pl.ds(at, span), :]
            query = stores[0][0][pl.ds(at, span), :]
            top = held[:, HS + 1 : HS + 2]
            finish(i, at, *online(query, top, held, [(keys, values)], 1024), EARLY)

        each(stores[0][0].shape[0], old_step)
    if last:
        late, at = refs[3], 0
        for side in range(2):
            for source in (stores[1][0], queries):
                count = source.shape[0] // 2
                late[at : at + count, :] = source[side * count : (side + 1) * count, :]
                at += count
    if last or not stores:
        seen = [(k, v) for _, k, v in stores] + [(keys, values)]
        fresh = late if last else queries

        def new_step(i, at):
            top = jnp.full((span, 1), -1e30, jnp.float32)
            held = jnp.zeros((span, LANES), jnp.float32)
            finish(i, at, *online(fresh[pl.ds(at, span), :], top, held, seen, 1024), LATE)

        each(fresh.shape[0], new_step)


def attend(packed, stores=(), state=None, me=None, blocks=0):
    fresh = sum(piece.shape[0] for piece in packed)
    old = sum(store[0].shape[0] for store in stores)
    last = me is not None
    total = old + fresh
    span = 1024
    kept_shapes = [(fresh, LANES), (LANES, fresh), (fresh, LANES)]
    vmem = pl.BlockSpec(memory_space=pltpu.VMEM)
    operands = list(packed) + [value for store in stores for value in store]
    operands += [state] if stores else []
    in_specs = [vmem] * len(operands)
    if last:
        operands, in_specs = [me] + operands, [pl.BlockSpec(memory_space=pltpu.SMEM)] + in_specs
        out_shape = jax.ShapeDtypeStruct((blocks, HS, 2 * HALF), jnp.bfloat16)
        scratch = [pltpu.VMEM(shape, jnp.bfloat16) for shape in kept_shapes]
        scratch.append(pltpu.VMEM((total - stores[0][0].shape[0], LANES), jnp.bfloat16))
        out_specs = vmem
    else:
        out_shape = [jax.ShapeDtypeStruct((old if stores else fresh, LANES), jnp.float32)]
        out_shape += [jax.ShapeDtypeStruct(shape, jnp.bfloat16) for shape in kept_shapes]
        scratch = []
        out_specs = [vmem] * 4
    return pl.pallas_call(
        functools.partial(
            attend_kernel, pieces=len(packed), olds=len(stores), last=last, span=span
        ),
        in_specs=in_specs,
        out_specs=out_specs,
        out_shape=out_shape,
        scratch_shapes=scratch,
        compiler_params=params(24),
        cost_estimate=cost(32 * total * total * LANES, 16 * total * LANES) if last else cost(1, 1),
        name="attend_heads",
    )(*operands)


def dispatch_kernel(
    me_ref, mixed_ref, near_ref, far_ref, rows_ref, gain_ref, label_ref, first_ref, send_ref, place_ref, mixed
):
    blocks, head, _ = mixed_ref.shape
    me = me_ref[0]
    x, y = me // 4, me // 2 % 2
    other = jnp.where(x % 2 == 0, x + 1, x - 1)
    columns = (x, other, 3 - x, 3 - other)
    for k in range(blocks):
        side = me % 2 if k < blocks // 2 else 1 - me % 2
        block = columns[k // 2 % 4] * 4 + (1 - y if k % 2 else y) * 2 + side
        mixed[k * head : (k + 1) * head, :] = mixed_ref[block]
    inner = near_ref.shape[0]
    first = dot_first(mixed[:inner, :], near_ref[...]) + dot_first(mixed[inner:, :], far_ref[...])
    first = rows_ref[...].astype(jnp.float32) + first
    first_ref[...] = first
    entry = rms_scale(first, gain_ref[...]).astype(jnp.bfloat16)
    keep, width = first.shape
    label = label_ref[...].astype(jnp.float32)
    across = jnp.broadcast_to(label, (keep, keep))
    same = (across == across.T) & (iota((keep, keep), 0) < iota((keep, keep), 1))
    slot = jnp.sum(jnp.where(same, 1.0, 0.0), axis=0, keepdims=True)
    place = (label * (2 * SLOTS) + slot).astype(jnp.int32)
    place_ref[...] = place
    places = send_ref.shape[0]
    half = width // 2
    row = iota((places, keep), 0)
    send = dot32(one_hot(row == place), entry[:, :half])
    send = send + dot32(one_hot(row == place + SLOTS), entry[:, half:])
    send_ref[...] = send.astype(jnp.bfloat16)


def dispatch(me, mixed, near, far, rows, gain, label, experts):
    keep, width = rows.shape
    places = experts * 2 * SLOTS
    vmem = pl.BlockSpec(memory_space=pltpu.VMEM)
    return pl.pallas_call(
        dispatch_kernel,
        in_specs=[pl.BlockSpec(memory_space=pltpu.SMEM)] + [vmem] * 6,
        scratch_shapes=[pltpu.VMEM((mixed.shape[0] * mixed.shape[1], keep), jnp.bfloat16)],
        out_shape=(
            jax.ShapeDtypeStruct((keep, width), jnp.float32),
            jax.ShapeDtypeStruct((places, width // 2), jnp.bfloat16),
            jax.ShapeDtypeStruct((1, keep), jnp.int32),
        ),
        compiler_params=params(24),
        cost_estimate=cost(8 * keep * near.size, 4 * near.size + 10 * keep * width),
        name="dispatch_rows",
    )(me, mixed, near, far, rows, gain, label)


def expert_kernel(slots_ref, w_in_ref, w_back_ref, out_ref, entry, hidden, total):
    count, half = slots_ref.shape
    pairs = count // 16
    low_side = iota((pairs, 8, half), 1) < SLOTS
    got = slots_ref[...].astype(jnp.float32).reshape(pairs, 2, 8, half)
    even, odd = got[:, 0], got[:, 1]
    low = jnp.where(low_side, even, pltpu.roll(odd, SLOTS, 1))
    high = jnp.where(low_side, pltpu.roll(even, SLOTS, 1), odd)
    entry[:, :half] = low.reshape(count // 2, half).astype(jnp.bfloat16)
    entry[:, half:] = high.reshape(count // 2, half).astype(jnp.bfloat16)
    tile = 256
    for at in range(0, hidden.shape[1], tile):
        part = dot32(entry[...], w_in_ref[:, at : at + tile])
        hidden[:, at : at + tile] = jnp.maximum(part, 0.0).astype(jnp.bfloat16)
    for at in range(0, total.shape[1], tile):
        total[:, at : at + tile] = dot32(hidden[...], w_back_ref[:, at : at + tile])
    low = total[:, :half].reshape(pairs, 8, half)
    high = total[:, half:].reshape(pairs, 8, half)
    even = jnp.where(low_side, low, pltpu.roll(high, SLOTS, 1))
    odd = jnp.where(low_side, pltpu.roll(low, SLOTS, 1), high)
    both = jnp.concatenate([even[:, None], odd[:, None]], axis=1)
    out_ref[...] = both.reshape(count, half).astype(jnp.bfloat16)


def run_expert(slots, w_in, w_back):
    count, half = slots.shape
    width, inner = w_in.shape
    vmem = pl.BlockSpec(memory_space=pltpu.VMEM)
    return pl.pallas_call(
        expert_kernel,
        in_specs=[vmem] * 3,
        out_specs=vmem,
        out_shape=jax.ShapeDtypeStruct((count, half), jnp.bfloat16),
        scratch_shapes=[
            pltpu.VMEM((count // 2, width), jnp.bfloat16),
            pltpu.VMEM((count // 2, inner), jnp.bfloat16),
            pltpu.VMEM((count // 2, width), jnp.float32),
        ],
        compiler_params=params(16),
        cost_estimate=cost(2 * count * w_in.size, 4 * w_in.size + 4 * slots.size),
        name="run_expert",
    )(slots, w_in, w_back)


def combine_kernel(back_ref, place_ref, first_ref, kept_ref, doc_ref, out_ref):
    back = back_ref[...]
    places, half = back.shape
    place = place_ref[...]
    keep = place.shape[1]
    row = iota((places, keep), 0)
    low = dot_first(one_hot(row == place), back)
    high = dot_first(one_hot(row == place + SLOTS), back)
    taken = jnp.concatenate([low, high], axis=1)
    second = (first_ref[...] + taken).astype(jnp.bfloat16)
    length = doc_ref.shape[0]
    spread = iota((length, keep), 0) == kept_ref[...] % length
    fresh = dot32(one_hot(spread), second).astype(jnp.bfloat16)
    hit = jnp.max(jnp.where(spread, 1.0, 0.0), axis=1, keepdims=True) > 0.5
    out_ref[...] = jnp.where(hit, fresh, doc_ref[...])


def combine(back, place, first, kept, document):
    keep, width = first.shape
    return pl.pallas_call(
        combine_kernel,
        out_shape=jax.ShapeDtypeStruct(document.shape, document.dtype),
        compiler_params=params(16),
        cost_estimate=cost(2 * keep * (2 * back.size + document.size), 6 * document.size),
        name="combine_rows",
    )(back, place, first, kept, document)


def body(
    tokens, kept, gain_attn, gain_ffn, w_query, w_key, w_value, w_out, expert_ids, w_in, w_back
):
    document = tokens[0]
    width = document.shape[1]
    ctx_count = lax.axis_size("ctx")
    experts = lax.axis_size("dp") * ctx_count
    me = lax.axis_index("ctx").astype(jnp.int32)[None]
    keep = kept.shape[1]

    def along(value, step):
        pairs = [(i, (i // 4 + step) % 4 * 4 + i % 4) for i in range(ctx_count)]
        return lax.ppermute(value, "ctx", pairs)

    def flip(value, bit):
        return lax.ppermute(value, "ctx", [(i, i ^ bit) for i in range(ctx_count)])

    heads = (w_query.T, w_key.T, w_value.T, w_out)
    me, kept = lax.optimization_barrier((me, kept))
    rows, normed, own_w, w_mine = gather_rows(kept, document, gain_attn[None], heads)

    b0, a1, a3 = flip(normed, 2), along(normed, 3), along(normed, 1)
    other_w = flip(own_w, 1)

    def trade(blocks):
        mine, theirs = project(blocks, own_w, other_w)
        return mine, flip(theirs, 1)

    own0, other0 = trade([normed])
    w_mine, own0 = lax.optimization_barrier((w_mine, own0))
    w_next = lax.ppermute(w_mine, ("dp", "ctx"), [(i, i ^ 18) for i in range(experts)])
    a3, a1, b0, w_next = lax.optimization_barrier((a3, a1, b0, w_next))
    low, high, left = (0, 0, HALF), (0, HALF, HALF), (1, HALF, HALF)
    count = w_out.shape[0]
    p1, p2, p3, w_pair = rearrange(
        [a3, a1, b0, w_mine, w_next],
        [(low, (2, 0, HALF)), (left, (2, 0, HALF)), (left, high), ((3, 0, count), (4, 0, count))],
    )
    a3, a1, b0, p1, p2, p3 = lax.optimization_barrier((a3, a1, b0, p1, p2, p3))
    r1, r2, r3 = along(p1, 1), along(p2, 3), flip(p3, 2)
    own1, other1 = trade([a3, a1, b0])
    state, *store = attend([own0, own1, other0, other1])
    r1, r2, r3, state = lax.optimization_barrier((r1, r2, r3, state))
    q1, q2 = rearrange([r1, r2], [((0, HALF, PART),), ((0, PART, HALF - PART), (1, 0, HALF))])
    r1, r2, r3, q1, q2 = lax.optimization_barrier((r1, r2, r3, q1, q2))
    t1, t2 = along(q1, 1), flip(q2, 2)
    own2, other2 = trade([r1, r2, r3])
    w_pair, own2 = lax.optimization_barrier((w_pair, own2))
    w_side = lax.ppermute(w_pair, "ctx", [(i, i ^ 4) for i in range(ctx_count)])
    state, *later = attend([own2, other2], [store], state)
    t1, t2, w_side, state = lax.optimization_barrier((t1, t2, w_side, state))
    own3, other3 = trade([t1, t2])
    (w_quad,) = rearrange([w_pair, w_side], [((0, 0, 2 * count), (1, 0, 2 * count))])
    w_rest = lax.ppermute(w_quad, "ctx", [(i, i ^ 12) for i in range(ctx_count)])
    mixed = attend([own3, other3], [store, later], state, me, ctx_count)
    w_quad, w_rest, mixed = lax.optimization_barrier((w_quad, w_rest, mixed))
    (w_near,) = rearrange([w_quad, w_rest], [((0, 0, 4 * count), (1, 0, 4 * count))])
    w_far = flip(w_near, 1)
    parts = lax.all_to_all(mixed, "ctx", split_axis=0, concat_axis=0, tiled=True)

    label = expert_ids[:, :, 0]
    first, send, place = dispatch(
        me, parts, w_near, w_far, rows, gain_ffn[None], label, experts
    )
    names = ("dp", "ctx")
    send = send.reshape(experts, 2 * SLOTS, width // 2)
    got = lax.all_to_all(send, names, split_axis=0, concat_axis=0, tiled=True)
    answer = run_expert(got.reshape(-1, width // 2), w_in[0], w_back[0])
    answer = answer.reshape(experts, 2 * SLOTS, width // 2)
    back = lax.all_to_all(answer, names, split_axis=0, concat_axis=0, tiled=True)
    return combine(back.reshape(-1, width // 2), place, first, kept, document)[None]


def solution(mesh):
    return jax.shard_map(
        body,
        mesh=mesh,
        in_specs=(
            P("dp", "ctx", None),
            P("dp", "ctx"),
            P(),
            P(),
            P(None, "ctx"),
            P(None, "ctx"),
            P(None, "ctx"),
            P("ctx", None),
            P("dp", "ctx", None),
            P(("dp", "ctx"), None, None),
            P(("dp", "ctx"), None, None),
        ),
        out_specs=P("dp", "ctx", None),
        check_vma=False,
    )
```

```python
import functools
import math

import jax
import jax.numpy as jnp
from jax import lax
from jax.experimental import pallas as pl
from jax.experimental.pallas import tpu as pltpu
from jax.sharding import PartitionSpec as P

HS = 64
LANES = 128
HALF = 128
SLOTS = 4
eps_norm = 1e-06
score_gain = 2.5
SCALE2 = score_gain / math.sqrt(HS) * math.log2(math.e)

A0, A1, A2, A3 = (0, 0), (1, 0), (2, 0), (3, 0)
B0, B1, B2, B3 = (0, 1), (1, 1), (2, 1), (3, 1)
EARLY = [(c, h) for c in (A0, A3, A1, B0) for h in (0, 1)]
LATE = [(A2, 0), (B3, 0), (A2, 1), (B1, 0), (B1, 1), (B3, 1), (B2, 0), (B2, 1)]
THIRD, REST = 48, 208


def params(limit):
    return pltpu.CompilerParams(vmem_limit_bytes=int(limit * 2**20))


def cost(flops, moved, exps=0):
    return pl.CostEstimate(flops=int(flops), bytes_accessed=int(moved), transcendentals=int(exps))


def dot32(a, b):
    return jnp.dot(a, b, preferred_element_type=jnp.float32)


def dot_first(a, b):
    return lax.dot_general(a, b, (((0,), (0,)), ((), ())), preferred_element_type=jnp.float32)


def iota(shape, axis):
    return lax.broadcasted_iota(jnp.int32, shape, axis)


def one_hot(flag):
    return jnp.where(flag, 1.0, 0.0).astype(jnp.bfloat16)


def rms_scale(values, gain):
    power = jnp.mean(values * values, axis=-1, keepdims=True)
    return values * lax.rsqrt(power + eps_norm) * gain


def gather_kernel(*refs):
    sources, (rows_hbm, normed_ref, w_ref, out_ref), (kept, doc, gain, rows_ref, sems) = refs[:7], refs[7:11], refs[11:]
    head = sources[3].shape[0]
    targets = [kept, doc, gain] + [w_ref.at[k * head : (k + 1) * head, :] for k in range(3)] + [out_ref]
    arrivals = [
        pltpu.make_async_copy(source, target, sems.at[k])
        for k, (source, target) in enumerate(zip(sources, targets))
    ]
    for arrival in arrivals:
        arrival.start()
    w_ref[3 * head :, :] = jnp.zeros((w_ref.shape[0] - 3 * head, w_ref.shape[1]), jnp.bfloat16)
    for arrival in arrivals:
        arrival.wait()
    length = doc.shape[0]
    spread = one_hot(iota((length, kept.shape[1]), 0) == kept[...] % length)
    rows = dot_first(spread, doc[...])
    rows_ref[...] = rows.astype(jnp.bfloat16)
    leaving = pltpu.make_async_copy(rows_ref, rows_hbm, sems.at[7])
    leaving.start()
    normed_ref[...] = rms_scale(rows, gain[...]).astype(jnp.bfloat16)
    leaving.wait()


def gather_rows(kept, document, gain, heads):
    keep, (_, width) = kept.shape[1], document.shape
    shape = jax.ShapeDtypeStruct((keep, width), jnp.bfloat16)
    vmem, hbm = pl.BlockSpec(memory_space=pltpu.VMEM), pl.BlockSpec(memory_space=pltpu.HBM)
    return pl.pallas_call(
        gather_kernel,
        in_specs=[hbm] * 7,
        out_specs=[hbm, vmem, vmem, vmem],
        out_shape=(
            shape,
            pltpu.VMEM(shape.shape, jnp.bfloat16),
            pltpu.VMEM((4 * HS, width), jnp.bfloat16),
            pltpu.VMEM(heads[3].shape, jnp.bfloat16),
        ),
        scratch_shapes=[
            pltpu.VMEM(kept.shape, jnp.int32),
            pltpu.VMEM(document.shape, jnp.bfloat16),
            pltpu.VMEM(gain.shape, jnp.float32),
            pltpu.VMEM(shape.shape, jnp.bfloat16),
            pltpu.SemaphoreType.DMA((8,)),
        ],
        compiler_params=params(62.5),
        cost_estimate=cost(2 * keep * document.size, 2 * (document.size + 2 * keep * width)),
        name="gather_rows",
    )(kept, document, gain, *heads)


def rearrange_kernel(*refs, recipes):
    sources, outs = refs[: len(refs) - len(recipes)], refs[len(refs) - len(recipes) :]
    for out, recipe in zip(outs, recipes):
        at = 0
        for which, start, size in recipe:
            out[at : at + size, :] = sources[which][start : start + size, :]
            at += size


def rearrange(sources, recipes):
    width = sources[0].shape[1]
    rows = [sum(size for _, _, size in recipe) for recipe in recipes]
    return pl.pallas_call(
        functools.partial(rearrange_kernel, recipes=recipes),
        out_shape=[jax.ShapeDtypeStruct((count, width), jnp.bfloat16) for count in rows],
        compiler_params=params(8),
        cost_estimate=cost(0, 4 * sum(rows) * width),
        name="rearrange_rows",
    )(*sources)


def dot_last(a, b):
    return lax.dot_general(a, b, (((1,), (1,)), ((), ())), preferred_element_type=jnp.float32)


def project_kernel(*refs):
    *blocks, own_w, other_w, own_ref, other_ref = refs
    at = 0
    for block in blocks:
        here = pl.ds(at, block.shape[0])
        value = block[...]
        own_ref[here, :] = dot_last(value, own_w[...]).astype(jnp.bfloat16)
        other_ref[here, :] = dot_last(value, other_w[...]).astype(jnp.bfloat16)
        at += block.shape[0]


def project(blocks, own_w, other_w):
    count = sum(block.shape[0] for block in blocks)
    columns = own_w.shape[0]
    shape = jax.ShapeDtypeStruct((count, columns), jnp.bfloat16)
    return pl.pallas_call(
        project_kernel,
        out_shape=(shape, shape),
        compiler_params=params(8),
        cost_estimate=cost(1, 1),
        name="project_rows",
    )(*blocks, own_w, other_w)


def unpack(packed, queries, keys, values):
    at = 0
    for piece in packed:
        count = piece.shape[0]
        here = pl.ds(at, count)
        pair = piece[:, :LANES].astype(jnp.float32)
        lane = iota((count, LANES), 1)
        twice = jnp.where(lane < HS, pair, pltpu.roll(pair, HS, 1)) * SCALE2
        high = twice.astype(jnp.bfloat16).astype(jnp.float32)
        queries[here, :] = jnp.where(lane < HS, high, twice - high).astype(jnp.bfloat16)
        turned = pair.T[HS:, :].astype(jnp.bfloat16)
        keys[:HS, here] = turned
        keys[HS:, here] = turned
        ones = jnp.where(lane == HS, 1.0, 0.0)
        values[here, :] = (piece[:, LANES:].astype(jnp.float32) + ones).astype(jnp.bfloat16)
        at += count


def chunks(total, size):
    size = total if total < 1600 else size
    return [(at, min(size, total - at)) for at in range(0, total, size)]


def online(query, top, held, stores, chunk):
    for keys, values in stores:
        for at, size in chunks(values.shape[0], chunk):
            scores = dot32(query, keys[:, at : at + size])
            newer = jnp.maximum(top, jnp.max(scores, axis=1, keepdims=True))
            weights = jnp.exp2(scores - newer).astype(jnp.bfloat16)
            held = held * jnp.exp2(top - newer) + dot32(weights, values[at : at + size, :])
            top = newer
    return top, held


def block_of(me, chip, side):
    dx, dy = chip
    x, y = me // 4, me // 2 % 2
    return (x + dx) % 4 * 4 + (1 - y if dy else y) * 2 + side


def attend_kernel(*refs, pieces, olds, last, span):
    refs = list(refs)
    me = refs.pop(0)[0] if last else None
    packed, refs = refs[:pieces], refs[pieces:]
    stores = []
    for _ in range(olds):
        stores.append(refs[:3])
        refs = refs[3:]
    state = refs.pop(0) if olds else None
    out = refs.pop(0)
    queries, keys, values = refs[:3]
    unpack(packed, queries, keys, values)

    def finish(side, at, top, held, units):
        if not last:
            lane = iota(held.shape, 1)
            out[pl.ds(at, span), :] = jnp.where(lane == HS + 1, top, held)
            return
        turned = held.T
        result = (turned[:HS] / turned[HS : HS + 1]).astype(jnp.bfloat16)
        core = me % 2
        side = jnp.where(side == 0, core, 1 - core)
        for k, (chip, half) in enumerate(units):
            out[block_of(me, chip, side), :, half * HALF : (half + 1) * HALF] = result[
                :, k * HALF : (k + 1) * HALF
            ]

    def each(total, step):
        def one(i, carry):
            step(i, pl.multiple_of(i * span, span))
            return carry

        if last:
            for i in range(total // span):
                step(i, i * span)
        else:
            lax.fori_loop(0, total // span, one, 0)

    if stores:

        def old_step(i, at):
            held = state[pl.ds(at, span), :]
            query = stores[0][0][pl.ds(at, span), :]
            top = held[:, HS + 1 : HS + 2]
            finish(i, at, *online(query, top, held, [(keys, values)], 1024), EARLY)

        each(stores[0][0].shape[0], old_step)
    if last:
        late, at = refs[3], 0
        for side in range(2):
            for source in (stores[1][0], queries):
                count = source.shape[0] // 2
                late[at : at + count, :] = source[side * count : (side + 1) * count, :]
                at += count
    if last or not stores:
        seen = [(k, v) for _, k, v in stores] + [(keys, values)]
        fresh = late if last else queries

        def new_step(i, at):
            top = jnp.full((span, 1), -1e30, jnp.float32)
            held = jnp.zeros((span, LANES), jnp.float32)
            finish(i, at, *online(fresh[pl.ds(at, span), :], top, held, seen, 1024), LATE)

        each(fresh.shape[0], new_step)


def attend(packed, stores=(), state=None, me=None, blocks=0):
    fresh = sum(piece.shape[0] for piece in packed)
    old = sum(store[0].shape[0] for store in stores)
    last = me is not None
    total = old + fresh
    span = 1024
    kept_shapes = [(fresh, LANES), (LANES, fresh), (fresh, LANES)]
    vmem = pl.BlockSpec(memory_space=pltpu.VMEM)
    operands = list(packed) + [value for store in stores for value in store]
    operands += [state] if stores else []
    in_specs = [vmem] * len(operands)
    if last:
        operands, in_specs = [me] + operands, [pl.BlockSpec(memory_space=pltpu.SMEM)] + in_specs
        out_shape = jax.ShapeDtypeStruct((blocks, HS, 2 * HALF), jnp.bfloat16)
        scratch = [pltpu.VMEM(shape, jnp.bfloat16) for shape in kept_shapes]
        scratch.append(pltpu.VMEM((total - stores[0][0].shape[0], LANES), jnp.bfloat16))
        out_specs = vmem
    else:
        out_shape = [jax.ShapeDtypeStruct((old if stores else fresh, LANES), jnp.float32)]
        out_shape += [jax.ShapeDtypeStruct(shape, jnp.bfloat16) for shape in kept_shapes]
        scratch = []
        out_specs = [vmem] * 4
    return pl.pallas_call(
        functools.partial(
            attend_kernel, pieces=len(packed), olds=len(stores), last=last, span=span
        ),
        in_specs=in_specs,
        out_specs=out_specs,
        out_shape=out_shape,
        scratch_shapes=scratch,
        compiler_params=params(24),
        cost_estimate=cost(32 * total * total * LANES, 16 * total * LANES) if last else cost(1, 1),
        name="attend_heads",
    )(*operands)


def dispatch_kernel(
    me_ref, mixed_ref, near_ref, far_ref, rows_ref, gain_ref, label_ref, first_ref, send_ref, place_ref, mixed
):
    blocks, head, _ = mixed_ref.shape
    me = me_ref[0]
    x, y = me // 4, me // 2 % 2
    other = jnp.where(x % 2 == 0, x + 1, x - 1)
    columns = (x, other, 3 - x, 3 - other)
    for k in range(blocks):
        side = me % 2 if k < blocks // 2 else 1 - me % 2
        block = columns[k // 2 % 4] * 4 + (1 - y if k % 2 else y) * 2 + side
        mixed[k * head : (k + 1) * head, :] = mixed_ref[block]
    inner = near_ref.shape[0]
    first = dot_first(mixed[:inner, :], near_ref[...]) + dot_first(mixed[inner:, :], far_ref[...])
    first = rows_ref[...].astype(jnp.float32) + first
    first_ref[...] = first
    entry = rms_scale(first, gain_ref[...]).astype(jnp.bfloat16)
    keep, width = first.shape
    label = label_ref[...].astype(jnp.float32)
    across = jnp.broadcast_to(label, (keep, keep))
    same = (across == across.T) & (iota((keep, keep), 0) < iota((keep, keep), 1))
    slot = jnp.sum(jnp.where(same, 1.0, 0.0), axis=0, keepdims=True)
    place = (label * (2 * SLOTS) + slot).astype(jnp.int32)
    place_ref[...] = place
    places = send_ref.shape[0]
    half = width // 2
    row = iota((places, keep), 0)
    send = dot32(one_hot(row == place), entry[:, :half])
    send = send + dot32(one_hot(row == place + SLOTS), entry[:, half:])
    send_ref[...] = send.astype(jnp.bfloat16)


def dispatch(me, mixed, near, far, rows, gain, label, experts):
    keep, width = rows.shape
    places = experts * 2 * SLOTS
    vmem = pl.BlockSpec(memory_space=pltpu.VMEM)
    return pl.pallas_call(
        dispatch_kernel,
        in_specs=[pl.BlockSpec(memory_space=pltpu.SMEM)] + [vmem] * 6,
        scratch_shapes=[pltpu.VMEM((mixed.shape[0] * mixed.shape[1], keep), jnp.bfloat16)],
        out_shape=(
            jax.ShapeDtypeStruct((keep, width), jnp.float32),
            jax.ShapeDtypeStruct((places, width // 2), jnp.bfloat16),
            jax.ShapeDtypeStruct((1, keep), jnp.int32),
        ),
        compiler_params=params(24),
        cost_estimate=cost(8 * keep * near.size, 4 * near.size + 10 * keep * width),
        name="dispatch_rows",
    )(me, mixed, near, far, rows, gain, label)


def expert_kernel(slots_ref, w_in_ref, w_back_ref, out_ref, entry, hidden, total):
    count, half = slots_ref.shape
    pairs = count // 16
    low_side = iota((pairs, 8, half), 1) < SLOTS
    got = slots_ref[...].astype(jnp.float32).reshape(pairs, 2, 8, half)
    even, odd = got[:, 0], got[:, 1]
    low = jnp.where(low_side, even, pltpu.roll(odd, SLOTS, 1))
    high = jnp.where(low_side, pltpu.roll(even, SLOTS, 1), odd)
    entry[:, :half] = low.reshape(count // 2, half).astype(jnp.bfloat16)
    entry[:, half:] = high.reshape(count // 2, half).astype(jnp.bfloat16)
    tile = 256
    for at in range(0, hidden.shape[1], tile):
        part = dot32(entry[...], w_in_ref[:, at : at + tile])
        hidden[:, at : at + tile] = jnp.maximum(part, 0.0).astype(jnp.bfloat16)
    for at in range(0, total.shape[1], tile):
        total[:, at : at + tile] = dot32(hidden[...], w_back_ref[:, at : at + tile])
    low = total[:, :half].reshape(pairs, 8, half)
    high = total[:, half:].reshape(pairs, 8, half)
    even = jnp.where(low_side, low, pltpu.roll(high, SLOTS, 1))
    odd = jnp.where(low_side, pltpu.roll(low, SLOTS, 1), high)
    both = jnp.concatenate([even[:, None], odd[:, None]], axis=1)
    out_ref[...] = both.reshape(count, half).astype(jnp.bfloat16)


def run_expert(slots, w_in, w_back):
    count, half = slots.shape
    width, inner = w_in.shape
    vmem = pl.BlockSpec(memory_space=pltpu.VMEM)
    return pl.pallas_call(
        expert_kernel,
        in_specs=[vmem] * 3,
        out_specs=vmem,
        out_shape=jax.ShapeDtypeStruct((count, half), jnp.bfloat16),
        scratch_shapes=[
            pltpu.VMEM((count // 2, width), jnp.bfloat16),
            pltpu.VMEM((count // 2, inner), jnp.bfloat16),
            pltpu.VMEM((count // 2, width), jnp.float32),
        ],
        compiler_params=params(16),
        cost_estimate=cost(2 * count * w_in.size, 4 * w_in.size + 4 * slots.size),
        name="run_expert",
    )(slots, w_in, w_back)


def combine_kernel(back_ref, place_ref, first_ref, kept_ref, doc_ref, out_ref):
    back = back_ref[...]
    places, half = back.shape
    place = place_ref[...]
    keep = place.shape[1]
    row = iota((places, keep), 0)
    low = dot_first(one_hot(row == place), back)
    high = dot_first(one_hot(row == place + SLOTS), back)
    taken = jnp.concatenate([low, high], axis=1)
    second = (first_ref[...] + taken).astype(jnp.bfloat16)
    length = doc_ref.shape[0]
    spread = iota((length, keep), 0) == kept_ref[...] % length
    fresh = dot32(one_hot(spread), second).astype(jnp.bfloat16)
    hit = jnp.max(jnp.where(spread, 1.0, 0.0), axis=1, keepdims=True) > 0.5
    out_ref[...] = jnp.where(hit, fresh, doc_ref[...])


def combine(back, place, first, kept, document):
    keep, width = first.shape
    return pl.pallas_call(
        combine_kernel,
        out_shape=jax.ShapeDtypeStruct(document.shape, document.dtype),
        compiler_params=params(16),
        cost_estimate=cost(2 * keep * (2 * back.size + document.size), 6 * document.size),
        name="combine_rows",
    )(back, place, first, kept, document)


def body(
    tokens, kept, gain_attn, gain_ffn, w_query, w_key, w_value, w_out, expert_ids, w_in, w_back
):
    document = tokens[0]
    width = document.shape[1]
    ctx_count = lax.axis_size("ctx")
    experts = lax.axis_size("dp") * ctx_count
    me = lax.axis_index("ctx").astype(jnp.int32)[None]
    keep = kept.shape[1]

    def along(value, step):
        pairs = [(i, (i // 4 + step) % 4 * 4 + i % 4) for i in range(ctx_count)]
        return lax.ppermute(value, "ctx", pairs)

    def flip(value, bit):
        return lax.ppermute(value, "ctx", [(i, i ^ bit) for i in range(ctx_count)])

    heads = (w_query.T, w_key.T, w_value.T, w_out)
    me, kept = lax.optimization_barrier((me, kept))
    rows, normed, own_w, w_mine = gather_rows(kept, document, gain_attn[None], heads)

    b0, a1, a3 = flip(normed, 2), along(normed, 3), along(normed, 1)
    other_w = flip(own_w, 1)

    def trade(blocks):
        mine, theirs = project(blocks, own_w, other_w)
        return mine, flip(theirs, 1)

    own0, other0 = trade([normed])
    w_mine, own0 = lax.optimization_barrier((w_mine, own0))
    w_next = lax.ppermute(w_mine, ("dp", "ctx"), [(i, i ^ 18) for i in range(experts)])
    a3, a1, b0, w_next, other0 = lax.optimization_barrier((a3, a1, b0, w_next, other0))
    low, high, left = (0, 0, HALF), (0, HALF, HALF), (1, HALF, HALF)
    count = w_out.shape[0]
    p1, p2, p3, w_pair = rearrange(
        [a3, a1, b0, w_mine, w_next],
        [(low, (2, 0, HALF)), (left, (2, 0, HALF)), (left, high), ((3, 0, count), (4, 0, count))],
    )
    a3, a1, b0, p1, p2, p3 = lax.optimization_barrier((a3, a1, b0, p1, p2, p3))
    r1, r2, r3 = along(p1, 1), along(p2, 3), flip(p3, 2)
    own1, other1 = trade([a3, a1, b0])
    state, *store = attend([own0, own1, other0, other1])
    r1, r2, r3, state = lax.optimization_barrier((r1, r2, r3, state))
    q1, q2, q3 = rearrange(
        [r1, r2, r3],
        [
            ((0, HALF, THIRD),),
            ((0, THIRD, HALF - THIRD), (1, 0, REST - HALF)),
            ((2, REST - HALF, keep - REST),),
        ],
    )
    r1, r2, r3, q1, q2, q3 = lax.optimization_barrier((r1, r2, r3, q1, q2, q3))
    t1, t2, t3 = along(q1, 1), flip(q2, 2), along(q3, 3)
    own2, other2 = trade([r1, r2, r3])
    w_pair, own2 = lax.optimization_barrier((w_pair, own2))
    w_side = lax.ppermute(w_pair, "ctx", [(i, i ^ 4) for i in range(ctx_count)])
    state, *later = attend([own2, other2], [store], state)
    t1, t2, t3, w_side, state = lax.optimization_barrier((t1, t2, t3, w_side, state))
    own3, other3 = trade([t1, t2, t3])
    (w_quad,) = rearrange([w_pair, w_side], [((0, 0, 2 * count), (1, 0, 2 * count))])
    w_rest = lax.ppermute(w_quad, "ctx", [(i, i ^ 12) for i in range(ctx_count)])
    mixed = attend([own3, other3], [store, later], state, me, ctx_count)
    w_quad, w_rest, mixed = lax.optimization_barrier((w_quad, w_rest, mixed))
    (w_near,) = rearrange([w_quad, w_rest], [((0, 0, 4 * count), (1, 0, 4 * count))])
    w_far = flip(w_near, 1)
    parts = lax.all_to_all(mixed, "ctx", split_axis=0, concat_axis=0, tiled=True)

    label = expert_ids[:, :, 0]
    first, send, place = dispatch(
        me, parts, w_near, w_far, rows, gain_ffn[None], label, experts
    )
    names = ("dp", "ctx")
    send = send.reshape(experts, 2 * SLOTS, width // 2)
    got = lax.all_to_all(send, names, split_axis=0, concat_axis=0, tiled=True)
    answer = run_expert(got.reshape(-1, width // 2), w_in[0], w_back[0])
    answer = answer.reshape(experts, 2 * SLOTS, width // 2)
    back = lax.all_to_all(answer, names, split_axis=0, concat_axis=0, tiled=True)
    return combine(back.reshape(-1, width // 2), place, first, kept, document)[None]


def solution(mesh):
    return jax.shard_map(
        body,
        mesh=mesh,
        in_specs=(
            P("dp", "ctx", None),
            P("dp", "ctx"),
            P(),
            P(),
            P(None, "ctx"),
            P(None, "ctx"),
            P(None, "ctx"),
            P("ctx", None),
            P("dp", "ctx", None),
            P(("dp", "ctx"), None, None),
            P(("dp", "ctx"), None, None),
        ),
        out_specs=P("dp", "ctx", None),
        check_vma=False,
    )
```
